512 devices in a mesh: samp: 8 (over z), pair: 16 (over y_lo, x), recv: 4 (over y_hi, core).
Axes of the slice: x: 4, y: 8 (y_hi: 2, y_lo: 4; y = y_hi * 4 + y_lo), z: 8, core: 2. Of those that a mesh axis runs over, the one named last changes fastest.
Arguments:
- cell_expression: bfloat16 [32, 16384, 2048], P('samp', 'recv', 'pair'), may hold values from 0 to 24
- cell_labels: int32 [32, 16384], P('samp', 'recv'), may hold values from 0 to 127, as said below
- ligand_gene: int32 [2048], P('pair'), may hold values from 0 to 2047
- receptor_gene: int32 [2048], P('pair'), may hold values from 0 to 2047
- pair_factor: bfloat16 [2048, 32], P('pair'), may hold values from -0.53033009 to 0.53033009
- sender_factor: bfloat16 [128, 32], replicated, may hold values from -0.5 to 0.5
- receiver_factor: bfloat16 [128, 32], P('recv'), may hold values from -2.5 to 2.5
Outputs:
- sample_factor: float32 [32, 32], P('samp')
The draws below stay inside these ranges and needn't reach their ends.
Inputs may be any that keep to these rules, and one draw needn't show every extreme that they name: `cell_labels`: in every sample one cell type has no cell.
All inputs are finite; a program needn't handle non-finite values.
Results may differ from the reference program's by a relative error of at most 0.0051.
Values may be sent and summed in bfloat16 or wider, within the bound.
No kernel may reach another device: no remote copies, remote signals or barrier semaphores. Data moves between devices by JAX's collectives and lax.ppermute only.
A program may use at most 64 MiB of HBM per device.

```python
import math
import jax
import jax.numpy as jnp
from jax import lax

CLUSTERS = 128
RANK = 32
SAMPLES = 32
CELLS = 16384
GENES = 2048
PAIRS = 2048
RECEIVER_BLOCK = 32


def rough_scale(key, shape):
    return jnp.exp(jax.random.uniform(key, shape, jnp.float32, -1.15, 1.15))


def draw_cell_expression(key, part):
    keys = jax.random.split(jax.random.fold_in(key, 101), 3)
    cell_scale = rough_scale(keys[0], (SAMPLES, CELLS, 1))
    gene_scale = rough_scale(keys[1], (1, 1, GENES))
    values = jax.random.uniform(keys[2], (SAMPLES, CELLS, GENES), jnp.float32, 0.0, 1.0)
    return (values * cell_scale * gene_scale).astype(jnp.bfloat16)


def draw_cell_labels(key, part):
    keys = jax.random.split(jax.random.fold_in(key, 202), 2)
    labels = jax.random.randint(keys[0], (SAMPLES, CELLS), 0, CLUSTERS, dtype=jnp.int32)
    absent = jax.random.randint(keys[1], (SAMPLES, 1), 0, CLUSTERS, dtype=jnp.int32)
    labels = jnp.where(labels == absent, (labels + 1) % CLUSTERS, labels)
    return labels.astype(jnp.int32)


def factor_rows(key, salt, rows):
    keys = jax.random.split(jax.random.fold_in(key, salt), 2)
    position = jnp.arange(rows, dtype=jnp.float32) / max(rows - 1, 1)
    scale = jnp.exp(math.log(3.0) * position)[:, None] * rough_scale(keys[0], (rows, 1)) * (0.5 / math.sqrt(rows))
    values = jax.random.truncated_normal(keys[1], -5.0, 5.0, (rows, RANK), jnp.float32)
    return (values * scale).astype(jnp.bfloat16)


def draw_pair_factor(key, part):
    return factor_rows(key, 303, PAIRS)


def draw_receiver_factor(key, part):
    return factor_rows(key, 404, CLUSTERS)


def place_ends(values, key, least, top_value):
    dims = values.shape
    spot = [jax.random.randint(jax.random.fold_in(key, axis), (), 0, dims[axis]) for axis in range(len(dims))]
    values = values.at[tuple(spot)].set(least)
    longest = dims.index(max(dims))
    spot[longest] = (spot[longest] + 1) % dims[longest]
    return values.at[tuple(spot)].set(top_value)


def normal_values(stream_key, shape, width, reach, kind=jnp.bfloat16):
    array = width * jax.random.normal(stream_key, shape, jnp.float32)
    return jnp.clip(array, min=-reach, max=reach).astype(kind)


def setup_inputs(seed: int = 0) -> dict:
    seeds = jax.random.split(jax.random.key(seed), 8)
    return {
        "cell_expression": draw_cell_expression(jax.random.fold_in(seeds[7], 71), 0),
        "cell_labels": draw_cell_labels(jax.random.fold_in(seeds[7], 71), 0),
        "ligand_gene": place_ends(jax.random.randint(seeds[2], (PAIRS,), 0, GENES), jax.random.fold_in(seeds[2], 1), 0, GENES - 1).astype(jnp.int32),
        "receptor_gene": place_ends(jax.random.randint(seeds[3], (PAIRS,), 0, GENES), jax.random.fold_in(seeds[3], 1), 0, GENES - 1).astype(jnp.int32),
        "pair_factor": draw_pair_factor(jax.random.fold_in(seeds[7], 71), 0),
        "sender_factor": normal_values(seeds[5], (CLUSTERS, RANK), CLUSTERS ** -0.5, 0.5),
        "receiver_factor": draw_receiver_factor(jax.random.fold_in(seeds[7], 71), 0),
    }


def reference(cell_expression, cell_labels, ligand_gene, receptor_gene, pair_factor, sender_factor, receiver_factor):
    cluster_ids = jnp.arange(CLUSTERS, dtype=jnp.int32)

    def per_sample(pieces):
        expression, labels = pieces
        member = (labels[:, None] == cluster_ids[None, :]).astype(jnp.bfloat16)
        totals = jnp.dot(expression.T.astype(jnp.float32), member.astype(jnp.float32), preferred_element_type=jnp.float32)
        counts = jnp.sum(member.astype(jnp.float32), axis=0)
        return (totals / jnp.maximum(counts, 1.0)[None, :]).astype(jnp.bfloat16)
    cluster_mean = lax.map(per_sample, (cell_expression, cell_labels))
    ligand_table = jnp.einsum('sga,ar->srg', cluster_mean.astype(jnp.float32), sender_factor.astype(jnp.float32)).astype(jnp.bfloat16)
    ligand_rows = ligand_table.astype(jnp.float32)[:, :, ligand_gene]
    receptor_total = jnp.zeros((SAMPLES, RANK, PAIRS), jnp.float32)
    for block_index in range(CLUSTERS // RECEIVER_BLOCK):
        lower = block_index * RECEIVER_BLOCK
        columns = cluster_mean[:, :, lower:lower + RECEIVER_BLOCK].astype(jnp.float32)
        weights = receiver_factor[lower:lower + RECEIVER_BLOCK].astype(jnp.float32)
        receptor_part = jnp.einsum('sgb,br->srg', columns, weights).astype(jnp.bfloat16)
        receptor_total = receptor_total + receptor_part.astype(jnp.float32)[:, :, receptor_gene]
    pair_weights = pair_factor.astype(jnp.float32).T
    product_total = jnp.sum(ligand_rows * receptor_total * pair_weights[None, :, :], axis=2)
    pair_gram = jnp.dot(pair_factor.T.astype(jnp.float32), pair_factor.astype(jnp.float32), preferred_element_type=jnp.float32)
    sender_gram = jnp.dot(sender_factor.T.astype(jnp.float32), sender_factor.astype(jnp.float32), preferred_element_type=jnp.float32)
    receiver_gram = jnp.dot(receiver_factor.T.astype(jnp.float32), receiver_factor.astype(jnp.float32), preferred_element_type=jnp.float32)
    hadamard = pair_gram * sender_gram * receiver_gram
    cholesky_factor = jnp.linalg.cholesky(hadamard)
    solution = jax.scipy.linalg.cho_solve((cholesky_factor, True), product_total.T)
    return solution.T
```

```python
import jax
import jax.numpy as jnp
from jax import lax
from jax.experimental import pallas as pl
from jax.experimental.pallas import tpu as pltpu
from jax.sharding import PartitionSpec as P

F32 = jnp.float32
BF16 = jnp.bfloat16
I32 = jnp.int32
LANES = 128
STEP_CELLS = 2048
SUB_CELLS = 512


def iota(shape, dim):
    return lax.broadcasted_iota(I32, shape, dim)


def totals_kernel(clusters, x_ref, labels_ref, receiver_ref, out_ref, count_ref):
    sample, step = pl.program_id(0), pl.program_id(1)
    genes = x_ref.shape[2]

    @pl.when(step == 0)
    def _():
        out_ref[0, :clusters, :] = jnp.zeros((clusters, genes), F32)
        count_ref[...] = jnp.zeros_like(count_ref)

    cells = x_ref.shape[1]
    kinds = iota((clusters, SUB_CELLS), 0)
    total = jnp.zeros((clusters, genes), F32)
    count = jnp.zeros((clusters, LANES), F32)
    for start in range(0, cells, SUB_CELLS):
        labels = labels_ref[pl.ds(sample, 1), start : start + SUB_CELLS]
        member = jnp.where(kinds == labels, 1.0, 0.0)
        for lane in range(0, SUB_CELLS, LANES):
            count = count + member[:, lane : lane + LANES]
        total = total + jnp.dot(
            member.astype(BF16), x_ref[0, start : start + SUB_CELLS, :], preferred_element_type=F32
        )
    out_ref[0, :clusters, :] += total
    count_ref[...] += count

    @pl.when(step == pl.num_programs(1) - 1)
    def _():
        row = lax.dot_general(
            jnp.ones((8, LANES), BF16),
            count_ref[...].astype(BF16),
            (((1,), (1,)), ((), ())),
            preferred_element_type=F32,
        )
        out_ref[0, clusters : clusters + 8, :] = row
        turned = receiver_ref[...].astype(F32).T
        rank, width = turned.shape
        parts = [turned[start : start + 8, :] for start in range(0, rank, 8)]
        out_ref[0, clusters + 8 : clusters + 16, :] = jnp.concatenate(parts, axis=1)


def tables_kernel(clusters, got_ref, sender_ref, weight_ref, ligand_ref, receptor_ref, out_ref, gram_ref):
    sources, _, genes = got_ref.shape
    rank = sender_ref.shape[0]
    width = clusters // sources
    total = jnp.sum(got_ref[:, :clusters, :], axis=0)
    row = jnp.sum(got_ref[:, clusters : clusters + 1, :], axis=0)
    count = jnp.broadcast_to(jnp.maximum(row, 1.0), (clusters, clusters)).T
    mean = (total / count).astype(BF16)
    blocks = []
    for source in range(sources):
        packed = got_ref[source, clusters + 8 : clusters + 16, :]
        parts = [packed[:, start : start + width] for start in range(0, LANES, width)]
        blocks.append(jnp.concatenate(parts, axis=0))
    receiver = jnp.concatenate(blocks, axis=1).astype(BF16)
    sender = sender_ref[...]
    tables = jnp.dot(jnp.concatenate([sender, receiver], axis=0), mean, preferred_element_type=F32)
    flat = (((1,), (1,)), ((), ()))
    sender_gram = lax.dot_general(sender, sender, flat, preferred_element_type=F32)
    receiver_gram = lax.dot_general(receiver, receiver, flat, preferred_element_type=F32)
    gram_ref[...] = sender_gram * receiver_gram
    ligand, receptor = ligand_ref[...], receptor_ref[...]
    rows = [ligand >> 7, ligand & 127, receptor >> 7, receptor & 127]
    where = jnp.zeros((16, LANES), F32)
    place = iota((16, LANES), 0)
    for spot, part in enumerate(rows):
        where = jnp.where(place == spot, part.astype(F32), where)
    block = jnp.concatenate([tables.astype(BF16), weight_ref[...], where.astype(BF16)], axis=0)
    for target in range(out_ref.shape[0]):
        out_ref[target] = block


def product_kernel(rank, got_ref, gram_ref, out_ref):
    sources = got_ref.shape[0]
    halves = sources // 2
    ligand_table = jnp.concatenate(
        [
            jnp.concatenate([got_ref[2 * h, :rank, :], got_ref[2 * h + 1, :rank, :]], axis=1)
            for h in range(halves)
        ],
        axis=0,
    )
    receptor_table = jnp.concatenate(
        [
            jnp.concatenate(
                [got_ref[2 * h, rank : 2 * rank, :], got_ref[2 * h + 1, rank : 2 * rank, :]], axis=1
            )
            for h in range(halves)
        ],
        axis=0,
    )
    spots = iota((2 * LANES, 2 * LANES), 0)

    def rows_of(table, high, low):
        upper = high >> 1
        lower = low + (high & 1) * LANES
        chosen = jnp.where(spots == lower, 1.0, 0.0).astype(BF16)
        spread = jnp.dot(table, chosen, preferred_element_type=F32)
        picked = jnp.zeros((rank, 2 * LANES), F32)
        for h in range(halves):
            picked = picked + jnp.where(upper == h, spread[h * rank : (h + 1) * rank, :], 0.0)
        return picked

    product = jnp.zeros((rank, 2 * LANES), F32)
    gram = jnp.zeros((rank, rank), F32)
    for h in range(halves):
        weight = jnp.concatenate(
            [got_ref[2 * h, 2 * rank : 3 * rank, :], got_ref[2 * h + 1, 2 * rank : 3 * rank, :]], axis=1
        )
        where = jnp.concatenate(
            [got_ref[2 * h, 3 * rank : 3 * rank + 16, :], got_ref[2 * h + 1, 3 * rank : 3 * rank + 16, :]],
            axis=1,
        ).astype(F32).astype(I32)
        ligand = rows_of(ligand_table, where[0:1, :], where[1:2, :])
        receptor = rows_of(receptor_table, where[2:3, :], where[3:4, :])
        product = product + ligand * receptor * weight.astype(F32)
        gram = gram + lax.dot_general(
            weight, weight, (((1,), (1,)), ((), ())), preferred_element_type=F32
        )
    right = jnp.sum(product, axis=1, keepdims=True)
    hadamard = gram * gram_ref[...]
    work = jnp.concatenate([hadamard, jnp.broadcast_to(right, (rank, LANES - rank))], axis=1)
    rows = iota((rank, LANES), 0)
    for j in range(rank):
        pivot = work[j : j + 1, j : j + 1]
        pivot = jnp.where(pivot > 0.0, pivot, jnp.nan)
        line = work[j : j + 1, :] / pivot
        work = jnp.where(rows == j, line, work - work[:, j : j + 1] * line)
    lanes = iota((rank, LANES), 1)
    answer = jnp.sum(jnp.where(rows == lanes, work[:, rank : rank + 1], 0.0), axis=0, keepdims=True)
    out_ref[...] = jnp.broadcast_to(answer[:, :rank], out_ref.shape)


def body(
    cell_expression,
    cell_labels,
    ligand_gene,
    receptor_gene,
    pair_factor,
    sender_factor,
    receiver_factor,
):
    samples, cells, genes = cell_expression.shape
    clusters, rank = sender_factor.shape
    targets = lax.axis_size("pair")
    height = clusters + 16
    step_cells = min(STEP_CELLS, cells)
    sent = pl.pallas_call(
        lambda *refs: totals_kernel(clusters, *refs),
        grid=(samples, cells // step_cells),
        in_specs=[
            pl.BlockSpec((1, step_cells, genes), lambda s, c: (s, c, 0)),
            pl.BlockSpec((samples, step_cells), lambda s, c: (0, c)),
            pl.BlockSpec(receiver_factor.shape, lambda s, c: (0, 0)),
        ],
        out_specs=pl.BlockSpec((1, height, genes), lambda s, c: (s, 0, 0)),
        out_shape=jax.ShapeDtypeStruct((samples, height, genes), F32),
        scratch_shapes=[pltpu.VMEM((clusters, LANES), F32)],
        name="totals",
    )(cell_expression, cell_labels, receiver_factor)
    got = lax.all_to_all(sent, "recv", 0, 0, tiled=True)
    sent, gram = pl.pallas_call(
        lambda *refs: tables_kernel(clusters, *refs),
        out_shape=(
            jax.ShapeDtypeStruct((targets, 3 * rank + 16, genes), BF16),
            jax.ShapeDtypeStruct((rank, rank), F32),
        ),
        name="tables",
    )(got, sender_factor.T, pair_factor.T, ligand_gene[None, :], receptor_gene[None, :])
    got = lax.all_to_all(sent, "pair", 0, 0, tiled=True)
    sent = pl.pallas_call(
        lambda *refs: product_kernel(rank, *refs),
        out_shape=jax.ShapeDtypeStruct((samples, rank), F32),
        name="product",
    )(got, gram)
    return lax.all_to_all(sent, "recv", 0, 0, tiled=True)


def solution(mesh):
    placed = (
        P("samp", "recv", "pair"),
        P("samp", "recv"),
        P("pair"),
        P("pair"),
        P("pair", None),
        P(),
        P("recv", None),
    )
    return jax.shard_map(
        body, mesh=mesh, in_specs=placed, out_specs=P("samp", None), check_vma=False
    )
```

```python
import jax
import jax.numpy as jnp
from jax import lax
from jax.experimental import pallas as pl
from jax.experimental.pallas import tpu as pltpu
from jax.sharding import Mesh
from jax.sharding import PartitionSpec as P

F32 = jnp.float32
BF16 = jnp.bfloat16
I32 = jnp.int32
LANES = 128
CHUNK = 512
ROW_PAIRS = (((1,), (1,)), ((), ()))


def iota(shape, dim):
    return lax.broadcasted_iota(I32, shape, dim)


def totals_kernel(
    x_hbm, labels_hbm, receiver_hbm, sender_hbm, weight_hbm, ligand_hbm, receptor_hbm,
    sums_ref, side_ref, sender_ref,
    x_ref, labels_ref, receiver_ref, weight_ref, ligand_ref, receptor_ref, x_sem, sems,
):
    samples, cells, genes = x_ref.shape
    rank, clusters = sender_ref.shape
    small = [
        pltpu.make_async_copy(source, target, sems.at[spot])
        for spot, (source, target) in enumerate(
            [
                (labels_hbm, labels_ref),
                (receiver_hbm, receiver_ref),
                (sender_hbm, sender_ref),
                (weight_hbm, weight_ref),
                (ligand_hbm, ligand_ref),
                (receptor_hbm, receptor_ref),
            ]
        )
    ]
    small[0].start()
    halves = [(0, samples // 2), (samples // 2, samples)]
    large = [
        pltpu.make_async_copy(x_hbm.at[pl.ds(a, b - a)], x_ref.at[pl.ds(a, b - a)], x_sem.at[i])
        for i, (a, b) in enumerate(halves)
    ]
    for copy in large:
        copy.start()
    for copy in small[1:]:
        copy.start()
    for copy in small:
        copy.wait()
    turned = receiver_ref[...].astype(F32).T
    parts = [turned[start : start + 8, :] for start in range(0, rank, 8)]
    packed = jnp.concatenate(parts, axis=1)
    side_ref[:rank, :] = weight_ref[...]
    ligand, receptor = ligand_ref[...], receptor_ref[...]
    digits = [ligand >> 7, ligand & 127, receptor >> 7, receptor & 127]
    place = iota((8, LANES), 0)
    where = jnp.zeros((8, LANES), F32)
    for spot, digit in enumerate(digits):
        where = jnp.where(place == spot, digit.astype(F32), where)
    side_ref[rank:, :] = where.astype(BF16)
    kinds = iota((clusters, CHUNK), 0).astype(F32).astype(BF16)
    one, zero = jnp.ones((), BF16), jnp.zeros((), BF16)
    for (first, last), copy in zip(halves, large):
        members = {}
        for sample in range(first, last):
            count = jnp.zeros((clusters, LANES), BF16)
            for start in range(0, cells, CHUNK):
                labels = labels_ref[sample : sample + 1, start : start + CHUNK].astype(F32)
                labels = jnp.broadcast_to(labels, (16, CHUNK)).astype(BF16)
                labels = jnp.concatenate([labels] * (clusters // 16), axis=0)
                member = jnp.where(kinds == labels, one, zero)
                for lane in range(0, CHUNK, LANES):
                    count = count + member[:, lane : lane + LANES]
                members[sample, start] = member
            row = lax.dot_general(
                jnp.ones((8, LANES), BF16), count, ROW_PAIRS, preferred_element_type=F32
            )
            sums_ref[sample, clusters : clusters + 8, :] = row
            sums_ref[sample, clusters + 8 :, :] = packed
        copy.wait()
        for sample in range(first, last):
            total = jnp.zeros((clusters, genes), F32)
            for start in range(0, cells, CHUNK):
                total = total + jnp.dot(
                    members[sample, start],
                    x_ref[sample, start : start + CHUNK, :],
                    preferred_element_type=F32,
                )
            sums_ref[sample, :clusters, :] = total


def tables_kernel(got_ref, sender_ref, side_ref, out_ref, gram_ref):
    sources = got_ref.shape[0]
    rank, clusters = sender_ref.shape
    targets, parts = out_ref.shape[0], rank // 8
    width = clusters // sources
    total = jnp.sum(got_ref[:, :clusters, :], axis=0)
    row = jnp.sum(got_ref[:, clusters : clusters + 1, :], axis=0)
    count = jnp.broadcast_to(jnp.maximum(row, 1.0), (clusters, clusters)).T
    mean = (total / count).astype(BF16)
    blocks = []
    for source in range(sources):
        packed = got_ref[source, clusters + 8 : clusters + 16, :]
        pieces = [packed[:, start : start + width] for start in range(0, LANES, width)]
        blocks.append(jnp.concatenate(pieces, axis=0))
    receiver = jnp.concatenate(blocks, axis=1).astype(BF16)
    sender = sender_ref[...]
    tables = jnp.dot(jnp.concatenate([sender, receiver], axis=0), mean, preferred_element_type=F32)
    side = side_ref[...]
    for part in range(parts):
        low = part * 8
        both = [tables[low : low + 8, :], tables[rank + low : rank + low + 8, :]]
        both = jnp.concatenate(both, axis=0).astype(BF16)
        for target in range(part * (targets // parts), (part + 1) * (targets // parts)):
            out_ref[target, :16, :] = both
            out_ref[target, 16:, :] = side
    sender_gram = lax.dot_general(sender, sender, ROW_PAIRS, preferred_element_type=F32)
    receiver_gram = lax.dot_general(receiver, receiver, ROW_PAIRS, preferred_element_type=F32)
    gram_ref[...] = sender_gram * receiver_gram


def product_kernel(rank, got_ref, out_ref):
    sources = got_ref.shape[0]
    part = lax.axis_index("part")
    tables = [got_ref[source, :16, :].astype(F32) for source in range(sources)]
    product = jnp.zeros((8, LANES), F32)
    for source in range(sources):
        weights = got_ref[source, 16 : 16 + rank, :].astype(F32)
        weight = weights[:8, :]
        for other in range(1, rank // 8):
            weight = jnp.where(part == other, weights[other * 8 : other * 8 + 8, :], weight)
        where = got_ref[source, 16 + rank : 24 + rank, :].astype(F32).astype(I32)
        digits = [jnp.broadcast_to(where[spot : spot + 1, :], (8, LANES)) for spot in range(4)]
        ligand = jnp.zeros((8, LANES), F32)
        receptor = jnp.zeros((8, LANES), F32)
        for block in range(sources):
            found = jnp.take_along_axis(tables[block][:8, :], digits[1], axis=1)
            ligand = jnp.where(digits[0] == block, found, ligand)
            found = jnp.take_along_axis(tables[block][8:, :], digits[3], axis=1)
            receptor = jnp.where(digits[2] == block, found, receptor)
        product = product + ligand * receptor * weight
    column = jnp.sum(product, axis=1, keepdims=True)
    line = jnp.where(iota((8, LANES), 0) == iota((8, LANES), 1), column, 0.0)
    line = jnp.sum(line, axis=0, keepdims=True)
    for target in range(out_ref.shape[0]):
        out_ref[target] = line


def inverse_kernel(got_ref, gram_ref, out_ref):
    rank = gram_ref.shape[0]
    gram = jnp.zeros((rank, rank), F32)
    for source in range(got_ref.shape[0]):
        weight = got_ref[source, 16 : 16 + rank, :]
        gram = gram + lax.dot_general(weight, weight, ROW_PAIRS, preferred_element_type=F32)
    hadamard = gram * gram_ref[...]
    rows, lanes = iota((rank, LANES), 0), iota((rank, LANES), 1)
    unit = jnp.where(iota((rank, LANES - rank), 0) == iota((rank, LANES - rank), 1), 1.0, 0.0)
    work = jnp.concatenate([hadamard, unit], axis=1)
    for j in range(rank):
        pivot = work[j : j + 1, j : j + 1]
        pivot = jnp.where(pivot > 0.0, pivot, jnp.nan)
        line = work[j : j + 1, :] / pivot
        work = jnp.where(rows == j, line, work - work[:, j : j + 1] * line)
    out_ref[...] = work[:, rank : 2 * rank]


def apply_kernel(samples, got_ref, inverse_ref, out_ref):
    rank = inverse_ref.shape[0]
    parts = got_ref.shape[0] // samples
    lines = []
    for sample in range(samples):
        pieces = [got_ref[part * samples + sample, :, :8] for part in range(parts)]
        lines.append(jnp.concatenate(pieces, axis=1))
    product = jnp.concatenate(lines + [jnp.zeros((8 - samples, rank), F32)], axis=0)
    answer = jnp.dot(
        product, inverse_ref[...], precision=lax.Precision.HIGHEST, preferred_element_type=F32
    )
    out_ref[...] = answer[:samples, :]


def on_chip(array):
    return pltpu.with_memory_space_constraint(array, pltpu.VMEM)


def body(
    cell_expression,
    cell_labels,
    ligand_gene,
    receptor_gene,
    pair_factor,
    sender_factor,
    receiver_factor,
):
    samples, cells, genes = cell_expression.shape
    clusters, rank = sender_factor.shape
    parts = lax.axis_size("part")
    targets = parts * lax.axis_size("line")
    anywhere = pl.BlockSpec(memory_space=pl.ANY)
    vmem = pl.BlockSpec(memory_space=pltpu.VMEM)
    sums, side, sender = pl.pallas_call(
        totals_kernel,
        in_specs=[anywhere] * 7,
        out_specs=(vmem, vmem, vmem),
        out_shape=(
            pltpu.VMEM((samples, clusters + 16, genes), F32),
            pltpu.VMEM((rank + 8, LANES), BF16),
            pltpu.VMEM((rank, clusters), BF16),
        ),
        scratch_shapes=[
            pltpu.VMEM((samples, cells, genes), BF16),
            pltpu.VMEM((samples, cells), I32),
            pltpu.VMEM(receiver_factor.shape, BF16),
            pltpu.VMEM((rank, LANES), BF16),
            pltpu.VMEM((1, LANES), I32),
            pltpu.VMEM((1, LANES), I32),
            pltpu.SemaphoreType.DMA((2,)),
            pltpu.SemaphoreType.DMA((6,)),
        ],
        name="totals",
    )(
        cell_expression,
        cell_labels,
        receiver_factor,
        sender_factor.T,
        pair_factor.T,
        ligand_gene[None, :],
        receptor_gene[None, :],
    )
    side, sender = on_chip(side), on_chip(sender)
    got = on_chip(lax.all_to_all(sums, "recv", 0, 0, tiled=True))
    sent, gram = pl.pallas_call(
        tables_kernel,
        in_specs=[vmem] * 3,
        out_specs=(vmem, vmem),
        out_shape=(
            pltpu.VMEM((targets, rank + 24, genes), BF16),
            pltpu.VMEM((rank, rank), F32),
        ),
        name="tables",
    )(got, sender, side)
    got = on_chip(lax.all_to_all(sent, ("part", "line"), 0, 0, tiled=True))
    sent = pl.pallas_call(
        lambda *refs: product_kernel(rank, *refs),
        in_specs=[vmem],
        out_specs=vmem,
        out_shape=pltpu.VMEM((parts * samples, 1, LANES), F32),
        name="product",
    )(got)
    final = on_chip(lax.all_to_all(sent, ("part", "recv"), 0, 0, tiled=True))
    inverse = pl.pallas_call(
        inverse_kernel,
        in_specs=[vmem] * 2,
        out_specs=vmem,
        out_shape=pltpu.VMEM((rank, rank), F32),
        name="inverse",
    )(got, on_chip(gram))
    return pl.pallas_call(
        lambda *refs: apply_kernel(samples, *refs),
        in_specs=[vmem] * 2,
        out_specs=vmem,
        out_shape=jax.ShapeDtypeStruct((samples, rank), F32),
        name="apply",
    )(final, on_chip(inverse))


def solution(mesh):
    samp, pair, recv = mesh.devices.shape
    split = Mesh(mesh.devices.reshape(samp, 4, pair // 4, recv), ("samp", "part", "line", "recv"))
    pairs = ("part", "line")
    placed = (
        P("samp", "recv", pairs),
        P("samp", "recv"),
        P(pairs),
        P(pairs),
        P(pairs, None),
        P(),
        P("recv", None),
    )
    return jax.shard_map(
        body, mesh=split, in_specs=placed, out_specs=P("samp", None), check_vma=False
    )
```

```python
import jax
import jax.numpy as jnp
from jax import lax
from jax.experimental import pallas as pl
from jax.experimental.pallas import tpu as pltpu
from jax.sharding import Mesh
from jax.sharding import PartitionSpec as P

F32 = jnp.float32
BF16 = jnp.bfloat16
I32 = jnp.int32
LANES = 128
CHUNK = 512
ROW_PAIRS = (((1,), (1,)), ((), ()))


def iota(shape, dim):
    return lax.broadcasted_iota(I32, shape, dim)


def totals_kernel(
    x_hbm, labels_hbm, receiver_hbm, sender_hbm, weight_hbm, ligand_hbm, receptor_hbm,
    sums_ref, side_ref, sender_ref,
    x_ref, labels_ref, receiver_ref, weight_ref, ligand_ref, receptor_ref, x_sem, sems,
):
    samples, cells, genes = x_ref.shape
    rank, clusters = sender_ref.shape
    small = [
        pltpu.make_async_copy(source, target, sems.at[spot])
        for spot, (source, target) in enumerate(
            [
                (labels_hbm, labels_ref),
                (receiver_hbm, receiver_ref),
                (sender_hbm, sender_ref),
                (weight_hbm, weight_ref),
                (ligand_hbm, ligand_ref),
                (receptor_hbm, receptor_ref),
            ]
        )
    ]
    small[0].start()
    halves = [(0, samples // 2), (samples // 2, samples)]
    large = [
        pltpu.make_async_copy(x_hbm.at[pl.ds(a, b - a)], x_ref.at[pl.ds(a, b - a)], x_sem.at[i])
        for i, (a, b) in enumerate(halves)
    ]
    for copy in large:
        copy.start()
    for copy in small[1:]:
        copy.start()
    small[0].wait()
    kinds = iota((clusters, CHUNK), 0).astype(F32).astype(BF16)
    one, zero = jnp.ones((), BF16), jnp.zeros((), BF16)
    extras = {}
    for (first, last), copy in zip(halves, large):
        members, counts = {}, {}
        for sample in range(first, last):
            count = jnp.zeros((clusters, LANES), BF16)
            for start in range(0, cells, CHUNK):
                labels = labels_ref[sample : sample + 1, start : start + CHUNK].astype(F32)
                labels = jnp.broadcast_to(labels, (16, CHUNK)).astype(BF16)
                labels = jnp.concatenate([labels] * (clusters // 16), axis=0)
                member = jnp.where(kinds == labels, one, zero)
                for lane in range(0, CHUNK, LANES):
                    count = count + member[:, lane : lane + LANES]
                members[sample, start] = member
            row = lax.dot_general(
                jnp.ones((8, LANES), BF16), count, ROW_PAIRS, preferred_element_type=F32
            ).astype(I32)
            row = jnp.where(iota((8, LANES), 0) == 0, row - (row & 255), row & 255)
            extras[sample] = row.astype(F32)
            counts[sample] = jnp.dot(
                count, jnp.ones((LANES, genes), BF16), preferred_element_type=F32
            )
        if first:
            for other in small[1:]:
                other.wait()
            fill_side(weight_ref, ligand_ref, receptor_ref, side_ref)
        copy.wait()
        for sample in range(first, last):
            total = jnp.zeros((clusters, genes), F32)
            for start in range(0, cells, CHUNK):
                total = total + jnp.dot(
                    members[sample, start],
                    x_ref[sample, start : start + CHUNK, :],
                    preferred_element_type=F32,
                )
            level = jnp.sum(total, axis=0, keepdims=True) * (1.0 / cells)
            level = level.astype(BF16).astype(F32)
            sums_ref[sample, :clusters, :] = (total - counts[sample] * level).astype(BF16)
            extras[sample] = jnp.where(iota((8, LANES), 0) == 2, level, extras[sample])
    turned = receiver_ref[...].astype(F32).T
    packed = jnp.concatenate([turned[start : start + 8, :] for start in range(0, rank, 8)], axis=1)
    for sample, extra in extras.items():
        sums_ref[sample, clusters:, :] = jnp.concatenate([extra, packed], axis=0).astype(BF16)


def fill_side(weight_ref, ligand_ref, receptor_ref, side_ref):
    rank = weight_ref.shape[0]
    parts = rank // 8
    weight = weight_ref[...]
    gram = lax.dot_general(weight, weight, ROW_PAIRS, preferred_element_type=F32)
    terms = []
    for _ in range(3):
        term = gram.astype(BF16).astype(F32)
        gram = gram - term
        terms += [term[8 * part : 8 * part + 8, 8 * part :] for part in range(parts)]
    terms = jnp.concatenate(terms, axis=1)
    terms = jnp.concatenate([terms, jnp.zeros((8, 2 * LANES - terms.shape[1]), F32)], axis=1)
    ligand, receptor = ligand_ref[...], receptor_ref[...]
    digits = [ligand >> 7, ligand & 127, receptor >> 7, receptor & 127]
    place = iota((8, LANES), 0)
    where = jnp.zeros((8, LANES), F32)
    for spot, digit in enumerate(digits):
        where = jnp.where(place == spot, digit.astype(F32), where)
    weight = weight.astype(F32)
    for part in range(parts):
        pieces = [weight[8 * part : 8 * part + 8, :], where, terms[:, :LANES], terms[:, LANES:]]
        side_ref[part] = jnp.concatenate(pieces, axis=0).astype(BF16)


def tables_kernel(got_ref, sender_ref, side_ref, out_ref, gram_ref):
    sources = got_ref.shape[0]
    rank, clusters = sender_ref.shape
    targets, parts = out_ref.shape[0], rank // 8
    width = clusters // sources
    extras = [got_ref[source, clusters:, :].astype(F32) for source in range(sources)]
    digits = jnp.concatenate([extra[:2, :] for extra in extras], axis=0).astype(BF16)
    levels = [jnp.broadcast_to(extra[2:3, :], (2, LANES)) for extra in extras]
    levels = jnp.concatenate(levels, axis=0).astype(BF16)
    levels = jnp.concatenate([levels, jnp.ones_like(levels)], axis=1)
    known = lax.dot_general(digits, levels, (((0,), (0,)), ((), ())), preferred_element_type=F32)
    count = jnp.maximum(known[:, LANES:], 1.0)
    total = known[:, :LANES] + jnp.sum(got_ref[:, :clusters, :].astype(F32), axis=0)
    mean = (total / count).astype(BF16)
    blocks = []
    for extra in extras:
        packed = extra[8:, :]
        pieces = [packed[:, start : start + width] for start in range(0, LANES, width)]
        blocks.append(jnp.concatenate(pieces, axis=0))
    receiver = jnp.concatenate(blocks, axis=1).astype(BF16)
    sender = sender_ref[...]
    tables = jnp.dot(jnp.concatenate([sender, receiver], axis=0), mean, preferred_element_type=F32)
    for part in range(parts):
        low = part * 8
        both = [tables[low : low + 8, :], tables[rank + low : rank + low + 8, :]]
        both = jnp.concatenate(both, axis=0).astype(BF16)
        side = side_ref[part]
        for target in range(part * (targets // parts), (part + 1) * (targets // parts)):
            out_ref[target, :16, :] = both
            out_ref[target, 16:, :] = side
    sender_gram = lax.dot_general(sender, sender, ROW_PAIRS, preferred_element_type=F32)
    receiver_gram = lax.dot_general(receiver, receiver, ROW_PAIRS, preferred_element_type=F32)
    gram_ref[...] = sender_gram * receiver_gram


def product_kernel(got_ref, out_ref):
    sources = got_ref.shape[0]
    tables = [got_ref[source, :16, :].astype(F32) for source in range(sources)]
    product = jnp.zeros((8, LANES), F32)
    for source in range(sources):
        side = got_ref[source, 16:32, :].astype(F32)
        where = side[8:, :].astype(I32)
        digits = [jnp.broadcast_to(where[spot : spot + 1, :], (8, LANES)) for spot in range(4)]
        ligand = jnp.zeros((8, LANES), F32)
        receptor = jnp.zeros((8, LANES), F32)
        for block in range(sources):
            found = jnp.take_along_axis(tables[block][:8, :], digits[1], axis=1)
            ligand = jnp.where(digits[0] == block, found, ligand)
            found = jnp.take_along_axis(tables[block][8:, :], digits[3], axis=1)
            receptor = jnp.where(digits[2] == block, found, receptor)
        product = product + ligand * receptor * side[:8, :]
    column = jnp.sum(product, axis=1, keepdims=True)
    line = jnp.where(iota((8, LANES), 0) == iota((8, LANES), 1), column, 0.0)
    line = jnp.sum(line, axis=0, keepdims=True)
    for target in range(out_ref.shape[0]):
        out_ref[target] = line


def inverse_kernel(got_ref, gram_ref, out_ref):
    rank = gram_ref.shape[0]
    parts = rank // 8
    terms = jnp.sum(got_ref[:, 32:, :].astype(F32), axis=0)
    terms = jnp.concatenate([terms[:8, :], terms[8:, :]], axis=1)
    wide = sum(range(8, rank + 8, 8))
    upper = terms[:, :wide] + terms[:, wide : 2 * wide] + terms[:, 2 * wide : 3 * wide]
    lines, start = [], 0
    for part in range(parts):
        width = rank - 8 * part
        line = upper[:, start : start + width]
        if part:
            line = jnp.concatenate([jnp.zeros((8, 8 * part), F32), line], axis=1)
        lines.append(line)
        start += width
    upper = jnp.concatenate(lines, axis=0)
    gram = jnp.where(iota((rank, rank), 0) <= iota((rank, rank), 1), upper, upper.T)
    hadamard = gram * gram_ref[...]
    rows = iota((rank, LANES), 0)
    unit = jnp.where(iota((rank, LANES - rank), 0) == iota((rank, LANES - rank), 1), 1.0, 0.0)
    work = jnp.concatenate([hadamard, unit], axis=1)
    for j in range(rank):
        pivot = work[j : j + 1, j : j + 1]
        pivot = jnp.where(pivot > 0.0, pivot, jnp.nan)
        line = work[j : j + 1, :] / pivot
        work = jnp.where(rows == j, line, work - work[:, j : j + 1] * line)
    out_ref[...] = work[:, rank : 2 * rank]


def apply_kernel(samples, got_ref, inverse_ref, out_ref):
    rank = inverse_ref.shape[0]
    parts = got_ref.shape[0] // samples
    lines = []
    for sample in range(samples):
        pieces = [got_ref[part * samples + sample, :, :8] for part in range(parts)]
        lines.append(jnp.concatenate(pieces, axis=1))
    product = jnp.concatenate(lines + [jnp.zeros((8 - samples, rank), F32)], axis=0)
    answer = jnp.dot(
        product, inverse_ref[...], precision=lax.Precision.HIGHEST, preferred_element_type=F32
    )
    out_ref[...] = answer[:samples, :]


def on_chip(array):
    return pltpu.with_memory_space_constraint(array, pltpu.VMEM)


def body(
    cell_expression,
    cell_labels,
    ligand_gene,
    receptor_gene,
    pair_factor,
    sender_factor,
    receiver_factor,
):
    samples, cells, genes = cell_expression.shape
    clusters, rank = sender_factor.shape
    parts = lax.axis_size("part")
    targets = parts * lax.axis_size("line")
    anywhere = pl.BlockSpec(memory_space=pl.ANY)
    vmem = pl.BlockSpec(memory_space=pltpu.VMEM)
    sums, side, sender = pl.pallas_call(
        totals_kernel,
        in_specs=[anywhere] * 7,
        out_specs=(vmem, vmem, vmem),
        out_shape=(
            pltpu.VMEM((samples, clusters + 16, genes), BF16),
            pltpu.VMEM((rank // 8, 32, LANES), BF16),
            pltpu.VMEM((rank, clusters), BF16),
        ),
        scratch_shapes=[
            pltpu.VMEM((samples, cells, genes), BF16),
            pltpu.VMEM((samples, cells), I32),
            pltpu.VMEM(receiver_factor.shape, BF16),
            pltpu.VMEM((rank, LANES), BF16),
            pltpu.VMEM((1, LANES), I32),
            pltpu.VMEM((1, LANES), I32),
            pltpu.SemaphoreType.DMA((2,)),
            pltpu.SemaphoreType.DMA((6,)),
        ],
        name="totals",
    )(
        cell_expression,
        cell_labels,
        receiver_factor,
        sender_factor.T,
        pair_factor.T,
        ligand_gene[None, :],
        receptor_gene[None, :],
    )
    side, sender = on_chip(side), on_chip(sender)
    got = on_chip(lax.all_to_all(sums, "recv", 0, 0, tiled=True))
    sent, gram = pl.pallas_call(
        tables_kernel,
        in_specs=[vmem] * 3,
        out_specs=(vmem, vmem),
        out_shape=(
            pltpu.VMEM((targets, 48, genes), BF16),
            pltpu.VMEM((rank, rank), F32),
        ),
        name="tables",
    )(got, sender, side)
    got = on_chip(lax.all_to_all(sent, ("part", "line"), 0, 0, tiled=True))
    sent = pl.pallas_call(
        product_kernel,
        in_specs=[vmem],
        out_specs=vmem,
        out_shape=pltpu.VMEM((parts * samples, 1, LANES), F32),
        name="product",
    )(got)
    final = on_chip(lax.all_to_all(on_chip(sent), ("part", "recv"), 0, 0, tiled=True))
    inverse = pl.pallas_call(
        inverse_kernel,
        in_specs=[vmem] * 2,
        out_specs=vmem,
        out_shape=pltpu.VMEM((rank, rank), F32),
        name="inverse",
    )(got, on_chip(gram))
    return pl.pallas_call(
        lambda *refs: apply_kernel(samples, *refs),
        in_specs=[vmem] * 2,
        out_specs=vmem,
        out_shape=jax.ShapeDtypeStruct((samples, rank), F32),
        name="apply",
    )(final, on_chip(inverse))


def solution(mesh):
    samp, pair, recv = mesh.devices.shape
    split = Mesh(mesh.devices.reshape(samp, 4, pair // 4, recv), ("samp", "part", "line", "recv"))
    pairs = ("part", "line")
    placed = (
        P("samp", "recv", pairs),
        P("samp", "recv"),
        P(pairs),
        P(pairs),
        P(pairs, None),
        P(),
        P("recv", None),
    )
    return jax.shard_map(
        body, mesh=split, in_specs=placed, out_specs=P("samp", None), check_vma=False
    )
```

```python
import jax
import jax.numpy as jnp
from jax import lax
from jax.experimental import pallas as pl
from jax.experimental.pallas import tpu as pltpu
from jax.sharding import Mesh
from jax.sharding import PartitionSpec as P

F32 = jnp.float32
BF16 = jnp.bfloat16
I32 = jnp.int32
LANES = 128
CHUNK = 512
ROW_PAIRS = (((1,), (1,)), ((), ()))


def iota(shape, dim):
    return lax.broadcasted_iota(I32, shape, dim)


def totals_kernel(
    x_hbm, labels_hbm, receiver_hbm, sender_hbm, weight_hbm, ligand_hbm, receptor_hbm,
    sums_ref, side_ref, sender_ref,
    x_ref, labels_ref, receiver_ref, weight_ref, ligand_ref, receptor_ref, x_sem, sems,
):
    samples, cells, genes = x_ref.shape
    rank, clusters = sender_ref.shape
    small = [
        pltpu.make_async_copy(source, target, sems.at[spot])
        for spot, (source, target) in enumerate(
            [
                (labels_hbm, labels_ref),
                (receiver_hbm, receiver_ref),
                (sender_hbm, sender_ref),
                (weight_hbm, weight_ref),
                (ligand_hbm, ligand_ref),
                (receptor_hbm, receptor_ref),
            ]
        )
    ]
    small[0].start()
    halves = [(0, samples // 2), (samples // 2, samples)]
    large = [
        pltpu.make_async_copy(x_hbm.at[pl.ds(a, b - a)], x_ref.at[pl.ds(a, b - a)], x_sem.at[i])
        for i, (a, b) in enumerate(halves)
    ]
    for copy in large:
        copy.start()
    for copy in small[1:]:
        copy.start()
    small[0].wait()
    kinds = iota((clusters, CHUNK), 0).astype(F32).astype(BF16)
    one, zero = jnp.ones((), BF16), jnp.zeros((), BF16)
    extras = {}
    for (first, last), copy in zip(halves, large):
        members, counts = {}, {}
        for sample in range(first, last):
            count = jnp.zeros((clusters, LANES), BF16)
            for start in range(0, cells, CHUNK):
                labels = labels_ref[sample : sample + 1, start : start + CHUNK].astype(F32)
                labels = jnp.broadcast_to(labels, (16, CHUNK)).astype(BF16)
                labels = jnp.concatenate([labels] * (clusters // 16), axis=0)
                member = jnp.where(kinds == labels, one, zero)
                for lane in range(0, CHUNK, LANES):
                    count = count + member[:, lane : lane + LANES]
                members[sample, start] = member
            row = lax.dot_general(
                jnp.ones((8, LANES), BF16), count, ROW_PAIRS, preferred_element_type=F32
            ).astype(I32)
            row = jnp.where(iota((8, LANES), 0) == 0, row - (row & 255), row & 255)
            extras[sample] = row.astype(F32)
            counts[sample] = jnp.dot(
                count, jnp.ones((LANES, genes), BF16), preferred_element_type=F32
            )
        if first:
            for other in small[1:]:
                other.wait()
            fill_side(weight_ref, ligand_ref, receptor_ref, side_ref)
        copy.wait()
        for sample in range(first, last):
            total = jnp.zeros((clusters, genes), F32)
            for start in range(0, cells, CHUNK):
                total = total + jnp.dot(
                    members[sample, start],
                    x_ref[sample, start : start + CHUNK, :],
                    preferred_element_type=F32,
                )
            level = jnp.sum(total, axis=0, keepdims=True) * (1.0 / cells)
            level = level.astype(BF16).astype(F32)
            sums_ref[sample, :clusters, :] = (total - counts[sample] * level).astype(BF16)
            extras[sample] = jnp.where(iota((8, LANES), 0) == 2, level, extras[sample])
    turned = receiver_ref[...].astype(F32).T
    packed = jnp.concatenate([turned[start : start + 8, :] for start in range(0, rank, 8)], axis=1)
    for sample, extra in extras.items():
        sums_ref[sample, clusters:, :] = jnp.concatenate([extra, packed], axis=0).astype(BF16)


def fill_side(weight_ref, ligand_ref, receptor_ref, side_ref):
    rank = weight_ref.shape[0]
    weight = weight_ref[...]
    gram = lax.dot_general(weight, weight, ROW_PAIRS, preferred_element_type=F32)
    terms = []
    for _ in range(3):
        term = gram.astype(BF16).astype(F32)
        gram = gram - term
        terms.append(term)
    terms = jnp.concatenate(terms + [jnp.zeros((rank, LANES - 3 * rank), F32)], axis=1)
    ligand, receptor = ligand_ref[...].astype(I32), receptor_ref[...].astype(I32)
    digits = [ligand >> 7, ligand & 127, receptor >> 7, receptor & 127]
    digits = [digit.astype(F32) for digit in digits]
    weight = weight.astype(F32)
    for piece in range(rank // 2):
        low = 8 * (2 * piece // 8)
        rows = [terms[2 * piece : 2 * piece + 2, :], jnp.zeros((2, LANES), F32)]
        rows = [weight[low : low + 8, :]] + digits + rows
        side_ref[piece] = jnp.concatenate(rows, axis=0).astype(BF16)


def tables_kernel(got_ref, sender_ref, side_ref, out_ref, gram_ref):
    sources = got_ref.shape[0]
    rank, clusters = sender_ref.shape
    targets, parts = out_ref.shape[0], rank // 8
    width = clusters // sources
    extras = [got_ref[source, clusters:, :].astype(F32) for source in range(sources)]
    digits = jnp.concatenate([extra[:2, :] for extra in extras], axis=0).astype(BF16)
    levels = [jnp.broadcast_to(extra[2:3, :], (2, LANES)) for extra in extras]
    levels = jnp.concatenate(levels, axis=0).astype(BF16)
    levels = jnp.concatenate([levels, jnp.ones_like(levels)], axis=1)
    known = lax.dot_general(digits, levels, (((0,), (0,)), ((), ())), preferred_element_type=F32)
    count = jnp.maximum(known[:, LANES:], 1.0)
    total = known[:, :LANES] + jnp.sum(got_ref[:, :clusters, :].astype(F32), axis=0)
    mean = (total / count).astype(BF16)
    blocks = []
    for extra in extras:
        packed = extra[8:, :]
        pieces = [packed[:, start : start + width] for start in range(0, LANES, width)]
        blocks.append(jnp.concatenate(pieces, axis=0))
    receiver = jnp.concatenate(blocks, axis=1).astype(BF16)
    sender = sender_ref[...]
    tables = jnp.dot(jnp.concatenate([sender, receiver], axis=0), mean, preferred_element_type=F32)
    own = lax.axis_index("recv")
    lines = targets // parts
    for part in range(parts):
        low = part * 8
        both = [tables[low : low + 8, :], tables[rank + low : rank + low + 8, :]]
        both = jnp.concatenate(both, axis=0).astype(BF16)
        for line in range(lines):
            out_ref[part * lines + line, :16, :] = both
            out_ref[part * lines + line, 16:, :] = side_ref[part * 4 + (line + own) % 4]
    sender_gram = lax.dot_general(sender, sender, ROW_PAIRS, preferred_element_type=F32)
    receiver_gram = lax.dot_general(receiver, receiver, ROW_PAIRS, preferred_element_type=F32)
    gram_ref[...] = sender_gram * receiver_gram


def choose(values, which):
    bit = 1
    while len(values) > 1:
        odd = (which & bit) != 0
        values = [jnp.where(odd, b, a) for a, b in zip(values[::2], values[1::2])]
        bit *= 2
    return values[0]


def product_kernel(rank, got_ref, out_ref):
    sources = got_ref.shape[0]
    tables = [got_ref[source, :16, :].astype(F32) for source in range(sources)]
    product = jnp.zeros((8, LANES), F32)
    terms = jnp.zeros((8, LANES), F32)
    for source in range(sources):
        side = got_ref[source, 16:32, :].astype(F32)
        terms = terms + side[8:, :]
        where = side[8:, :].astype(I32)
        digits = [jnp.broadcast_to(where[spot : spot + 1, :], (8, LANES)) for spot in range(4)]
        ligand = [jnp.take_along_axis(table[:8, :], digits[1], axis=1) for table in tables]
        receptor = [jnp.take_along_axis(table[8:, :], digits[3], axis=1) for table in tables]
        ligand, receptor = choose(ligand, digits[0]), choose(receptor, digits[2])
        product = product + ligand * receptor * side[:8, :]
    column = jnp.sum(product, axis=1, keepdims=True)
    rows, lanes = iota((8, LANES), 0), iota((8, LANES), 1)
    own = lax.axis_index("recv")
    spot = (lax.axis_index("line") + own) % 4
    gram = terms[4:6, :rank] + terms[4:6, rank : 2 * rank] + terms[4:6, 2 * rank : 3 * rank]
    gram = jnp.concatenate([gram, jnp.zeros((2, LANES - rank), F32)], axis=1)
    gram = jnp.concatenate([gram] * 4, axis=0)
    tile = jnp.where(rows >> 1 == spot, gram, 0.0)
    tile = jnp.where(lanes == rank + own, column, tile)
    for target in range(out_ref.shape[0]):
        out_ref[target] = tile


def solve_kernel(samples, got_ref, gram_ref, out_ref):
    rank = gram_ref.shape[0]
    parts = rank // 8
    scale = jnp.concatenate([gram_ref[...], jnp.ones((rank, LANES - rank), F32)], axis=1)
    work = []
    for part in range(parts):
        block = got_ref[part * samples]
        for sample in range(1, samples):
            block = block + got_ref[part * samples + sample]
        work.append(block * scale[8 * part : 8 * part + 8, :])
    rows = iota((8, LANES), 0)
    for part in range(parts):
        columns = [
            [jnp.broadcast_to(block[:, lane : lane + 1], (8, LANES)) for block in work]
            for lane in range(8 * part, 8 * part + 8)
        ]
        lead, inner = work[part], [column[part] for column in columns]
        for row in range(8):
            pivot = inner[row][row : row + 1, :]
            pivot = jnp.where(pivot > 0.0, 1.0 / pivot, jnp.nan)
            here, times = rows == row, inner[row]
            line = lead[row : row + 1, :] * pivot
            lead = jnp.where(here, line, lead - times * line)
            for later in range(row + 1, 8):
                line = inner[later][row : row + 1, :] * pivot
                inner[later] = jnp.where(here, line, inner[later] - times * line)
        for other in range(parts):
            if other == part:
                work[other] = lead
            else:
                for row in range(8):
                    work[other] = work[other] - columns[row][other] * lead[row : row + 1, :]
    answer = jnp.concatenate(work, axis=0)[:, rank : rank + 8].T
    out_ref[...] = answer[:samples, :]


def on_chip(array):
    return pltpu.with_memory_space_constraint(array, pltpu.VMEM)


def body(
    cell_expression,
    cell_labels,
    ligand_gene,
    receptor_gene,
    pair_factor,
    sender_factor,
    receiver_factor,
):
    samples, cells, genes = cell_expression.shape
    clusters, rank = sender_factor.shape
    parts = lax.axis_size("part")
    targets = parts * lax.axis_size("line")
    anywhere = pl.BlockSpec(memory_space=pl.ANY)
    vmem = pl.BlockSpec(memory_space=pltpu.VMEM)
    sums, side, sender = pl.pallas_call(
        totals_kernel,
        in_specs=[anywhere] * 7,
        out_specs=(vmem, vmem, vmem),
        out_shape=(
            pltpu.VMEM((samples, clusters + 16, genes), BF16),
            pltpu.VMEM((rank // 2, 16, LANES), BF16),
            pltpu.VMEM((rank, clusters), BF16),
        ),
        scratch_shapes=[
            pltpu.VMEM((samples, cells, genes), BF16),
            pltpu.VMEM((samples, cells), I32),
            pltpu.VMEM(receiver_factor.shape, BF16),
            pltpu.VMEM((rank, LANES), BF16),
            pltpu.VMEM((1, LANES), I32),
            pltpu.VMEM((1, LANES), I32),
            pltpu.SemaphoreType.DMA((2,)),
            pltpu.SemaphoreType.DMA((6,)),
        ],
        name="totals",
    )(
        cell_expression,
        cell_labels,
        receiver_factor,
        sender_factor.T,
        pair_factor.T,
        ligand_gene[None, :],
        receptor_gene[None, :],
    )
    side, sender = on_chip(side), on_chip(sender)
    got = on_chip(lax.all_to_all(sums, "recv", 0, 0, tiled=True))
    sent, gram = pl.pallas_call(
        tables_kernel,
        in_specs=[vmem] * 3,
        out_specs=(vmem, vmem),
        out_shape=(
            pltpu.VMEM((targets, 32, genes), BF16),
            pltpu.VMEM((rank, rank), F32),
        ),
        name="tables",
    )(got, sender, side)
    got = on_chip(lax.all_to_all(sent, ("part", "line"), 0, 0, tiled=True))
    sent = pl.pallas_call(
        lambda *refs: product_kernel(rank, *refs),
        in_specs=[vmem],
        out_specs=vmem,
        out_shape=pltpu.VMEM((parts * samples, 8, LANES), F32),
        name="product",
    )(got)
    got = on_chip(lax.all_to_all(sent, ("part", "recv"), 0, 0, tiled=True))
    return pl.pallas_call(
        lambda *refs: solve_kernel(samples, *refs),
        in_specs=[vmem] * 2,
        out_specs=vmem,
        out_shape=jax.ShapeDtypeStruct((samples, rank), F32),
        name="solve",
    )(got, on_chip(gram))


def solution(mesh):
    samp, pair, recv = mesh.devices.shape
    split = Mesh(mesh.devices.reshape(samp, 4, pair // 4, recv), ("samp", "part", "line", "recv"))
    pairs = ("part", "line")
    placed = (
        P("samp", "recv", pairs),
        P("samp", "recv"),
        P(pairs),
        P(pairs),
        P(pairs, None),
        P(),
        P("recv", None),
    )
    return jax.shard_map(
        body, mesh=split, in_specs=placed, out_specs=P("samp", None), check_vma=False
    )
```

```python
import jax
import jax.numpy as jnp
from jax import lax
from jax.experimental import pallas as pl
from jax.experimental.pallas import tpu as pltpu
from jax.sharding import Mesh
from jax.sharding import PartitionSpec as P

F32 = jnp.float32
BF16 = jnp.bfloat16
I32 = jnp.int32
LANES = 128
CHUNK = 512
ROW_PAIRS = (((1,), (1,)), ((), ()))


def iota(shape, dim):
    return lax.broadcasted_iota(I32, shape, dim)


def totals_kernel(
    x_hbm, labels_hbm, receiver_hbm, sender_hbm, weight_hbm, ligand_hbm, receptor_hbm,
    sums_ref, side_ref, sender_ref,
    x_ref, labels_ref, receiver_ref, weight_ref, ligand_ref, receptor_ref, x_sem, sems,
):
    samples, cells, genes = x_ref.shape
    rank, clusters = sender_ref.shape
    small = [
        pltpu.make_async_copy(source, target, sems.at[spot])
        for spot, (source, target) in enumerate(
            [
                (labels_hbm, labels_ref),
                (receiver_hbm, receiver_ref),
                (sender_hbm, sender_ref),
                (weight_hbm, weight_ref),
                (ligand_hbm, ligand_ref),
                (receptor_hbm, receptor_ref),
            ]
        )
    ]
    for copy in small:
        copy.start()
    spans = [(sample, sample + 1) for sample in range(samples)]
    large = [
        pltpu.make_async_copy(x_hbm.at[pl.ds(a, b - a)], x_ref.at[pl.ds(a, b - a)], x_sem.at[i])
        for i, (a, b) in enumerate(spans)
    ]
    for spot, copy in enumerate(large):
        copy.start(priority=min(spot, 1))
    small[0].wait()
    kinds = iota((clusters, CHUNK), 0).astype(F32).astype(BF16)
    one, zero = jnp.ones((), BF16), jnp.zeros((), BF16)
    for other in small[1:]:
        other.wait()
    fill_side(weight_ref, ligand_ref, receptor_ref, side_ref)
    extras = {}
    for (first, last), copy in zip(spans, large):
        members, counts = {}, {}
        for sample in range(first, last):
            count = jnp.zeros((clusters, LANES), BF16)
            for start in range(0, cells, CHUNK):
                labels = labels_ref[sample : sample + 1, start : start + CHUNK].astype(F32)
                labels = jnp.broadcast_to(labels, (16, CHUNK)).astype(BF16)
                labels = jnp.concatenate([labels] * (clusters // 16), axis=0)
                member = jnp.where(kinds == labels, one, zero)
                for lane in range(0, CHUNK, LANES):
                    count = count + member[:, lane : lane + LANES]
                members[sample, start] = member
            row = lax.dot_general(
                jnp.ones((8, LANES), BF16), count, ROW_PAIRS, preferred_element_type=F32
            ).astype(I32)
            row = jnp.where(iota((8, LANES), 0) == 0, row - (row & 255), row & 255)
            extras[sample] = row.astype(F32)
            counts[sample] = jnp.dot(
                count, jnp.ones((LANES, genes), BF16), preferred_element_type=F32
            )
        copy.wait()
        for sample in range(first, last):
            total = jnp.zeros((clusters, genes), F32)
            for start in range(0, cells, CHUNK):
                total = total + jnp.dot(
                    members[sample, start],
                    x_ref[sample, start : start + CHUNK, :],
                    preferred_element_type=F32,
                )
            level = jnp.sum(total, axis=0, keepdims=True) * (1.0 / cells)
            level = level.astype(BF16).astype(F32)
            sums_ref[sample, :clusters, :] = (total - counts[sample] * level).astype(BF16)
            extras[sample] = jnp.where(iota((8, LANES), 0) == 2, level, extras[sample])
    turned = receiver_ref[...].astype(F32).T
    packed = jnp.concatenate([turned[start : start + 8, :] for start in range(0, rank, 8)], axis=1)
    for sample, extra in extras.items():
        sums_ref[sample, clusters:, :] = jnp.concatenate([extra, packed], axis=0).astype(BF16)


def fill_side(weight_ref, ligand_ref, receptor_ref, side_ref):
    rank = weight_ref.shape[0]
    weight = weight_ref[...]
    gram = lax.dot_general(weight, weight, ROW_PAIRS, preferred_element_type=F32)
    terms = []
    for _ in range(3):
        term = gram.astype(BF16).astype(F32)
        gram = gram - term
        terms.append(term)
    terms = jnp.concatenate(terms + [jnp.zeros((rank, LANES - 3 * rank), F32)], axis=1)
    ligand, receptor = ligand_ref[...].astype(I32), receptor_ref[...].astype(I32)
    digits = [ligand >> 7, ligand & 127, receptor >> 7, receptor & 127]
    digits = [digit.astype(F32) for digit in digits]
    weight = weight.astype(F32)
    for piece in range(rank // 2):
        low = 8 * (2 * piece // 8)
        rows = [terms[2 * piece : 2 * piece + 2, :], jnp.zeros((2, LANES), F32)]
        rows = [weight[low : low + 8, :]] + digits + rows
        side_ref[piece] = jnp.concatenate(rows, axis=0).astype(BF16)


def tables_kernel(got_ref, sender_ref, side_ref, out_ref, gram_ref):
    sources = got_ref.shape[0]
    rank, clusters = sender_ref.shape
    targets, parts = out_ref.shape[0], rank // 8
    width = clusters // sources
    extras = [got_ref[source, clusters:, :].astype(F32) for source in range(sources)]
    digits = jnp.concatenate([extra[:2, :] for extra in extras], axis=0).astype(BF16)
    levels = [jnp.broadcast_to(extra[2:3, :], (2, LANES)) for extra in extras]
    levels = jnp.concatenate(levels, axis=0).astype(BF16)
    levels = jnp.concatenate([levels, jnp.ones_like(levels)], axis=1)
    known = lax.dot_general(digits, levels, (((0,), (0,)), ((), ())), preferred_element_type=F32)
    count = jnp.maximum(known[:, LANES:], 1.0)
    total = known[:, :LANES] + jnp.sum(got_ref[:, :clusters, :].astype(F32), axis=0)
    mean = (total / count).astype(BF16)
    blocks = []
    for extra in extras:
        packed = extra[8:, :]
        pieces = [packed[:, start : start + width] for start in range(0, LANES, width)]
        blocks.append(jnp.concatenate(pieces, axis=0))
    receiver = jnp.concatenate(blocks, axis=1).astype(BF16)
    sender = sender_ref[...]
    tables = jnp.dot(jnp.concatenate([sender, receiver], axis=0), mean, preferred_element_type=F32)
    own = lax.axis_index("recv")
    lines = targets // parts
    for part in range(parts):
        low = part * 8
        both = [tables[low : low + 8, :], tables[rank + low : rank + low + 8, :]]
        both = jnp.concatenate(both, axis=0).astype(BF16)
        for line in range(lines):
            out_ref[part * lines + line, :16, :] = both
            out_ref[part * lines + line, 16:, :] = side_ref[part * 4 + (line + own) % 4]
    sender_gram = lax.dot_general(sender, sender, ROW_PAIRS, preferred_element_type=F32)
    receiver_gram = lax.dot_general(receiver, receiver, ROW_PAIRS, preferred_element_type=F32)
    gram_ref[...] = sender_gram * receiver_gram


def choose(values, which):
    bit = 1
    while len(values) > 1:
        odd = (which & bit) != 0
        values = [jnp.where(odd, b, a) for a, b in zip(values[::2], values[1::2])]
        bit *= 2
    return values[0]


def product_kernel(rank, got_ref, out_ref):
    sources = got_ref.shape[0]
    tables = [got_ref[source, :16, :].astype(F32) for source in range(sources)]
    product = jnp.zeros((8, LANES), F32)
    terms = jnp.zeros((8, LANES), F32)
    for source in range(sources):
        side = got_ref[source, 16:32, :].astype(F32)
        terms = terms + side[8:, :]
        where = side[8:, :].astype(I32)
        digits = [jnp.broadcast_to(where[spot : spot + 1, :], (8, LANES)) for spot in range(4)]
        ligand = [jnp.take_along_axis(table[:8, :], digits[1], axis=1) for table in tables]
        receptor = [jnp.take_along_axis(table[8:, :], digits[3], axis=1) for table in tables]
        ligand, receptor = choose(ligand, digits[0]), choose(receptor, digits[2])
        product = product + ligand * receptor * side[:8, :]
    column = jnp.sum(product, axis=1, keepdims=True)
    rows, lanes = iota((8, LANES), 0), iota((8, LANES), 1)
    own = lax.axis_index("recv")
    spot = (lax.axis_index("line") + own) % 4
    gram = terms[4:6, :rank] + terms[4:6, rank : 2 * rank] + terms[4:6, 2 * rank : 3 * rank]
    gram = jnp.concatenate([gram, jnp.zeros((2, LANES - rank), F32)], axis=1)
    gram = jnp.concatenate([gram] * 4, axis=0)
    tile = jnp.where(rows >> 1 == spot, gram, 0.0)
    tile = jnp.where(lanes == rank + own, column, tile)
    for target in range(out_ref.shape[0]):
        out_ref[target] = tile


def solve_kernel(samples, got_ref, gram_ref, out_ref):
    rank = gram_ref.shape[0]
    parts = rank // 8
    scale = jnp.concatenate([gram_ref[...], jnp.ones((rank, LANES - rank), F32)], axis=1)
    work = []
    for part in range(parts):
        block = got_ref[part * samples]
        for sample in range(1, samples):
            block = block + got_ref[part * samples + sample]
        work.append(block * scale[8 * part : 8 * part + 8, :])
    rows = iota((8, LANES), 0)
    for part in range(parts):
        columns = [
            [jnp.broadcast_to(block[:, lane : lane + 1], (8, LANES)) for block in work]
            for lane in range(8 * part, 8 * part + 8)
        ]
        lead, inner = work[part], [column[part] for column in columns]
        for row in range(8):
            pivot = inner[row][row : row + 1, :]
            pivot = jnp.where(pivot > 0.0, 1.0 / pivot, jnp.nan)
            here, times = rows == row, inner[row]
            line = lead[row : row + 1, :] * pivot
            lead = jnp.where(here, line, lead - times * line)
            for later in range(row + 1, 8):
                line = inner[later][row : row + 1, :] * pivot
                inner[later] = jnp.where(here, line, inner[later] - times * line)
        for other in range(parts):
            if other == part:
                work[other] = lead
            else:
                for row in range(8):
                    work[other] = work[other] - columns[row][other] * lead[row : row + 1, :]
    answer = jnp.concatenate(work, axis=0)[:, rank : rank + 8].T
    out_ref[...] = answer[:samples, :]


def on_chip(array):
    return pltpu.with_memory_space_constraint(array, pltpu.VMEM)


def body(
    cell_expression,
    cell_labels,
    ligand_gene,
    receptor_gene,
    pair_factor,
    sender_factor,
    receiver_factor,
):
    samples, cells, genes = cell_expression.shape
    clusters, rank = sender_factor.shape
    parts = lax.axis_size("part")
    targets = parts * lax.axis_size("line")
    anywhere = pl.BlockSpec(memory_space=pl.ANY)
    vmem = pl.BlockSpec(memory_space=pltpu.VMEM)
    sums, side, sender = pl.pallas_call(
        totals_kernel,
        in_specs=[anywhere] * 7,
        out_specs=(vmem, vmem, vmem),
        out_shape=(
            pltpu.VMEM((samples, clusters + 16, genes), BF16),
            pltpu.VMEM((rank // 2, 16, LANES), BF16),
            pltpu.VMEM((rank, clusters), BF16),
        ),
        scratch_shapes=[
            pltpu.VMEM((samples, cells, genes), BF16),
            pltpu.VMEM((samples, cells), I32),
            pltpu.VMEM(receiver_factor.shape, BF16),
            pltpu.VMEM((rank, LANES), BF16),
            pltpu.VMEM((1, LANES), I32),
            pltpu.VMEM((1, LANES), I32),
            pltpu.SemaphoreType.DMA((samples,)),
            pltpu.SemaphoreType.DMA((6,)),
        ],
        name="totals",
    )(
        cell_expression,
        cell_labels,
        receiver_factor,
        sender_factor.T,
        pair_factor.T,
        ligand_gene[None, :],
        receptor_gene[None, :],
    )
    side, sender = on_chip(side), on_chip(sender)
    got = on_chip(lax.all_to_all(sums, "recv", 0, 0, tiled=True))
    sent, gram = pl.pallas_call(
        tables_kernel,
        in_specs=[vmem] * 3,
        out_specs=(vmem, vmem),
        out_shape=(
            pltpu.VMEM((targets, 32, genes), BF16),
            pltpu.VMEM((rank, rank), F32),
        ),
        name="tables",
    )(got, sender, side)
    got = on_chip(lax.all_to_all(sent, ("part", "line"), 0, 0, tiled=True))
    sent = pl.pallas_call(
        lambda *refs: product_kernel(rank, *refs),
        in_specs=[vmem],
        out_specs=vmem,
        out_shape=pltpu.VMEM((parts * samples, 8, LANES), F32),
        name="product",
    )(got)
    got = on_chip(lax.all_to_all(sent, ("part", "recv"), 0, 0, tiled=True))
    return pl.pallas_call(
        lambda *refs: solve_kernel(samples, *refs),
        in_specs=[vmem] * 2,
        out_specs=vmem,
        out_shape=jax.ShapeDtypeStruct((samples, rank), F32),
        name="solve",
    )(got, on_chip(gram))


def solution(mesh):
    samp, pair, recv = mesh.devices.shape
    split = Mesh(mesh.devices.reshape(samp, 4, pair // 4, recv), ("samp", "part", "line", "recv"))
    pairs = ("part", "line")
    placed = (
        P("samp", "recv", pairs),
        P("samp", "recv"),
        P(pairs),
        P(pairs),
        P(pairs, None),
        P(),
        P("recv", None),
    )
    return jax.shard_map(
        body, mesh=split, in_specs=placed, out_specs=P("samp", None), check_vma=False
    )
```

```python
import jax
import jax.numpy as jnp
from jax import lax
from jax.experimental import pallas as pl
from jax.experimental.pallas import tpu as pltpu
from jax.sharding import Mesh
from jax.sharding import PartitionSpec as P

F32 = jnp.float32
BF16 = jnp.bfloat16
I32 = jnp.int32
LANES = 128
CHUNK = 512
ROW_PAIRS = (((1,), (1,)), ((), ()))


def iota(shape, dim):
    return lax.broadcasted_iota(I32, shape, dim)


def totals_kernel(
    x_hbm, labels_hbm, receiver_hbm, sender_hbm, weight_hbm, ligand_hbm, receptor_hbm,
    sums_ref, side_ref, sender_ref,
    x_ref, labels_ref, receiver_ref, weight_ref, ligand_ref, receptor_ref, x_sem, sems,
):
    samples, cells, genes = x_ref.shape
    rank, clusters = sender_ref.shape
    small = [
        pltpu.make_async_copy(source, target, sems.at[spot])
        for spot, (source, target) in enumerate(
            [
                (labels_hbm, labels_ref),
                (receiver_hbm, receiver_ref),
                (sender_hbm, sender_ref),
                (weight_hbm, weight_ref),
                (ligand_hbm, ligand_ref),
                (receptor_hbm, receptor_ref),
            ]
        )
    ]
    for copy in small:
        copy.start()
    spans = [(sample, sample + 1) for sample in range(samples)]
    large = [
        pltpu.make_async_copy(x_hbm.at[pl.ds(a, b - a)], x_ref.at[pl.ds(a, b - a)], x_sem.at[i])
        for i, (a, b) in enumerate(spans)
    ]
    for spot, copy in enumerate(large):
        copy.start(priority=min(spot, 1))
    small[0].wait()
    kinds = iota((clusters, CHUNK), 0).astype(F32).astype(BF16)
    one, zero = jnp.ones((), BF16), jnp.zeros((), BF16)
    for other in small[1:]:
        other.wait()
    fill_side(weight_ref, ligand_ref, receptor_ref, side_ref)
    extras = {}
    for (first, last), copy in zip(spans, large):
        members, counts = {}, {}
        for sample in range(first, last):
            count = jnp.zeros((clusters, LANES), BF16)
            for start in range(0, cells, CHUNK):
                labels = labels_ref[sample : sample + 1, start : start + CHUNK].astype(F32)
                labels = jnp.broadcast_to(labels, (16, CHUNK)).astype(BF16)
                labels = jnp.concatenate([labels] * (clusters // 16), axis=0)
                member = jnp.where(kinds == labels, one, zero)
                for lane in range(0, CHUNK, LANES):
                    count = count + member[:, lane : lane + LANES]
                members[sample, start] = member
            row = lax.dot_general(
                jnp.ones((8, LANES), BF16), count, ROW_PAIRS, preferred_element_type=F32
            ).astype(I32)
            row = jnp.where(iota((8, LANES), 0) == 0, row - (row & 255), row & 255)
            extras[sample] = row.astype(F32)
            counts[sample] = jnp.dot(
                count, jnp.ones((LANES, genes), BF16), preferred_element_type=F32
            )
        copy.wait()
        for sample in range(first, last):
            total = jnp.zeros((clusters, genes), F32)
            for start in range(0, cells, CHUNK):
                total = total + jnp.dot(
                    members[sample, start],
                    x_ref[sample, start : start + CHUNK, :],
                    preferred_element_type=F32,
                )
            level = jnp.sum(total, axis=0, keepdims=True) * (1.0 / cells)
            level = level.astype(BF16).astype(F32)
            sums_ref[sample, :clusters, :] = (total - counts[sample] * level).astype(BF16)
            extras[sample] = jnp.where(iota((8, LANES), 0) == 2, level, extras[sample])
    turned = receiver_ref[...].astype(F32).T
    packed = jnp.concatenate([turned[start : start + 8, :] for start in range(0, rank, 8)], axis=1)
    for sample, extra in extras.items():
        sums_ref[sample, clusters:, :] = jnp.concatenate([extra, packed], axis=0).astype(BF16)


def fill_side(weight_ref, ligand_ref, receptor_ref, side_ref):
    rank = weight_ref.shape[0]
    weight = weight_ref[...]
    gram = lax.dot_general(weight, weight, ROW_PAIRS, preferred_element_type=F32)
    terms = []
    for _ in range(3):
        term = gram.astype(BF16).astype(F32)
        gram = gram - term
        terms.append(term)
    terms = jnp.concatenate(terms + [jnp.zeros((rank, LANES - 3 * rank), F32)], axis=1)
    ligand, receptor = ligand_ref[...].astype(I32), receptor_ref[...].astype(I32)
    digits = [ligand >> 7, ligand & 127, receptor >> 7, receptor & 127]
    digits = [digit.astype(F32) for digit in digits]
    weight = weight.astype(F32)
    for piece in range(rank // 2):
        low = 8 * (2 * piece // 8)
        rows = [terms[2 * piece : 2 * piece + 2, :], jnp.zeros((2, LANES), F32)]
        rows = [weight[low : low + 8, :]] + digits + rows
        side_ref[piece] = jnp.concatenate(rows, axis=0).astype(BF16)


def tables_kernel(got_ref, sender_ref, side_ref, out_ref, gram_ref):
    sources = got_ref.shape[0]
    rank, clusters = sender_ref.shape
    targets, parts = out_ref.shape[0], rank // 8
    width = clusters // sources
    extras = [got_ref[source, clusters:, :].astype(F32) for source in range(sources)]
    digits = jnp.concatenate([extra[:2, :] for extra in extras], axis=0).astype(BF16)
    levels = [jnp.broadcast_to(extra[2:3, :], (2, LANES)) for extra in extras]
    levels = jnp.concatenate(levels, axis=0).astype(BF16)
    levels = jnp.concatenate([levels, jnp.ones_like(levels)], axis=1)
    known = lax.dot_general(digits, levels, (((0,), (0,)), ((), ())), preferred_element_type=F32)
    count = jnp.maximum(known[:, LANES:], 1.0)
    total = known[:, :LANES] + jnp.sum(got_ref[:, :clusters, :].astype(F32), axis=0)
    mean = (total / count).astype(BF16)
    blocks = []
    for extra in extras:
        packed = extra[8:, :]
        pieces = [packed[:, start : start + width] for start in range(0, LANES, width)]
        blocks.append(jnp.concatenate(pieces, axis=0))
    receiver = jnp.concatenate(blocks, axis=1).astype(BF16)
    sender = sender_ref[...]
    tables = jnp.dot(jnp.concatenate([sender, receiver], axis=0), mean, preferred_element_type=F32)
    own = lax.axis_index("recv")
    lines = targets // parts
    for part in range(parts):
        low = part * 8
        both = [tables[low : low + 8, :], tables[rank + low : rank + low + 8, :]]
        both = jnp.concatenate(both, axis=0).astype(BF16)
        for line in range(lines):
            out_ref[line * parts + part, :16, :] = both
            out_ref[line * parts + part, 16:, :] = side_ref[part * 4 + (line + own) % 4]
    sender_gram = lax.dot_general(sender, sender, ROW_PAIRS, preferred_element_type=F32)
    receiver_gram = lax.dot_general(receiver, receiver, ROW_PAIRS, preferred_element_type=F32)
    gram_ref[...] = sender_gram * receiver_gram


def choose(values, which):
    bit = 1
    while len(values) > 1:
        odd = (which & bit) != 0
        values = [jnp.where(odd, b, a) for a, b in zip(values[::2], values[1::2])]
        bit *= 2
    return values[0]


def product_kernel(rank, got_ref, out_ref):
    sources = got_ref.shape[0]
    order = [line * 4 + part for part in range(4) for line in range(sources // 4)]
    tables = [got_ref[source, :16, :].astype(F32) for source in order]
    product = jnp.zeros((8, LANES), F32)
    terms = jnp.zeros((8, LANES), F32)
    for source in range(sources):
        side = got_ref[source, 16:32, :].astype(F32)
        terms = terms + side[8:, :]
        where = side[8:, :].astype(I32)
        digits = [jnp.broadcast_to(where[spot : spot + 1, :], (8, LANES)) for spot in range(4)]
        ligand = [jnp.take_along_axis(table[:8, :], digits[1], axis=1) for table in tables]
        receptor = [jnp.take_along_axis(table[8:, :], digits[3], axis=1) for table in tables]
        ligand, receptor = choose(ligand, digits[0]), choose(receptor, digits[2])
        product = product + ligand * receptor * side[:8, :]
    column = jnp.sum(product, axis=1, keepdims=True)
    rows, lanes = iota((8, LANES), 0), iota((8, LANES), 1)
    own = lax.axis_index("recv")
    spot = (lax.axis_index("line") + own) % 4
    gram = terms[4:6, :rank] + terms[4:6, rank : 2 * rank] + terms[4:6, 2 * rank : 3 * rank]
    gram = jnp.concatenate([gram, jnp.zeros((2, LANES - rank), F32)], axis=1)
    gram = jnp.concatenate([gram] * 4, axis=0)
    tile = jnp.where(rows >> 1 == spot, gram, 0.0)
    tile = jnp.where(lanes == rank + own, column, tile)
    for target in range(out_ref.shape[0]):
        out_ref[target] = tile


def solve_kernel(samples, got_ref, gram_ref, out_ref):
    rank = gram_ref.shape[0]
    parts = rank // 8
    scale = jnp.concatenate([gram_ref[...], jnp.ones((rank, LANES - rank), F32)], axis=1)
    work = []
    for part in range(parts):
        block = got_ref[part * samples]
        for sample in range(1, samples):
            block = block + got_ref[part * samples + sample]
        work.append(block * scale[8 * part : 8 * part + 8, :])
    rows = iota((8, LANES), 0)
    for part in range(parts):
        columns = [
            [jnp.broadcast_to(block[:, lane : lane + 1], (8, LANES)) for block in work]
            for lane in range(8 * part, 8 * part + 8)
        ]
        lead, inner = work[part], [column[part] for column in columns]
        for row in range(8):
            pivot = inner[row][row : row + 1, :]
            pivot = jnp.where(pivot > 0.0, 1.0 / pivot, jnp.nan)
            here, times = rows == row, inner[row]
            line = lead[row : row + 1, :] * pivot
            lead = jnp.where(here, line, lead - times * line)
            for later in range(row + 1, 8):
                line = inner[later][row : row + 1, :] * pivot
                inner[later] = jnp.where(here, line, inner[later] - times * line)
        for other in range(parts):
            if other == part:
                work[other] = lead
            else:
                for row in range(8):
                    work[other] = work[other] - columns[row][other] * lead[row : row + 1, :]
    answer = jnp.concatenate(work, axis=0)[:, rank : rank + 8].T
    out_ref[...] = answer[:samples, :]


def on_chip(array):
    return pltpu.with_memory_space_constraint(array, pltpu.VMEM)


def body(
    cell_expression,
    cell_labels,
    ligand_gene,
    receptor_gene,
    pair_factor,
    sender_factor,
    receiver_factor,
):
    samples, cells, genes = cell_expression.shape
    clusters, rank = sender_factor.shape
    parts = lax.axis_size("part")
    targets = parts * lax.axis_size("line")
    anywhere = pl.BlockSpec(memory_space=pl.ANY)
    vmem = pl.BlockSpec(memory_space=pltpu.VMEM)
    sums, side, sender = pl.pallas_call(
        totals_kernel,
        in_specs=[anywhere] * 7,
        out_specs=(vmem, vmem, vmem),
        out_shape=(
            pltpu.VMEM((samples, clusters + 16, genes), BF16),
            pltpu.VMEM((rank // 2, 16, LANES), BF16),
            pltpu.VMEM((rank, clusters), BF16),
        ),
        scratch_shapes=[
            pltpu.VMEM((samples, cells, genes), BF16),
            pltpu.VMEM((samples, cells), I32),
            pltpu.VMEM(receiver_factor.shape, BF16),
            pltpu.VMEM((rank, LANES), BF16),
            pltpu.VMEM((1, LANES), I32),
            pltpu.VMEM((1, LANES), I32),
            pltpu.SemaphoreType.DMA((samples,)),
            pltpu.SemaphoreType.DMA((6,)),
        ],
        name="totals",
    )(
        cell_expression,
        cell_labels,
        receiver_factor,
        sender_factor.T,
        pair_factor.T,
        ligand_gene[None, :],
        receptor_gene[None, :],
    )
    side, sender = on_chip(side), on_chip(sender)
    got = on_chip(lax.all_to_all(sums, "recv", 0, 0, tiled=True))
    sent, gram = pl.pallas_call(
        tables_kernel,
        in_specs=[vmem] * 3,
        out_specs=(vmem, vmem),
        out_shape=(
            pltpu.VMEM((targets, 32, genes), BF16),
            pltpu.VMEM((rank, rank), F32),
        ),
        name="tables",
    )(got, sender, side)
    got = on_chip(lax.all_to_all(sent, ("line", "part"), 0, 0, tiled=True))
    sent = pl.pallas_call(
        lambda *refs: product_kernel(rank, *refs),
        in_specs=[vmem],
        out_specs=vmem,
        out_shape=pltpu.VMEM((parts * samples, 8, LANES), F32),
        name="product",
    )(got)
    got = on_chip(lax.all_to_all(sent, ("part", "recv"), 0, 0, tiled=True))
    return pl.pallas_call(
        lambda *refs: solve_kernel(samples, *refs),
        in_specs=[vmem] * 2,
        out_specs=vmem,
        out_shape=jax.ShapeDtypeStruct((samples, rank), F32),
        name="solve",
    )(got, on_chip(gram))


def solution(mesh):
    samp, pair, recv = mesh.devices.shape
    split = Mesh(mesh.devices.reshape(samp, 4, pair // 4, recv), ("samp", "part", "line", "recv"))
    pairs = ("part", "line")
    placed = (
        P("samp", "recv", pairs),
        P("samp", "recv"),
        P(pairs),
        P(pairs),
        P(pairs, None),
        P(),
        P("recv", None),
    )
    return jax.shard_map(
        body, mesh=split, in_specs=placed, out_specs=P("samp", None), check_vma=False
    )
```

```python
import jax
import jax.numpy as jnp
from jax import lax
from jax.experimental import pallas as pl
from jax.experimental.pallas import tpu as pltpu
from jax.sharding import Mesh
from jax.sharding import PartitionSpec as P

F32 = jnp.float32
BF16 = jnp.bfloat16
I32 = jnp.int32
LANES = 128
CHUNK = 512
ROW_PAIRS = (((1,), (1,)), ((), ()))


def iota(shape, dim):
    return lax.broadcasted_iota(I32, shape, dim)


def totals_kernel(
    x_hbm, labels_hbm, receiver_hbm, sender_hbm, weight_hbm, ligand_hbm, receptor_hbm,
    sums_ref, side_ref, sender_ref,
    x_ref, labels_ref, receiver_ref, weight_ref, ligand_ref, receptor_ref, x_sem, sems,
):
    samples, cells, genes = x_ref.shape
    rank, clusters = sender_ref.shape
    small = [
        pltpu.make_async_copy(source, target, sems.at[spot])
        for spot, (source, target) in enumerate(
            [
                (labels_hbm, labels_ref),
                (receiver_hbm, receiver_ref),
                (sender_hbm, sender_ref),
                (weight_hbm, weight_ref),
                (ligand_hbm, ligand_ref),
                (receptor_hbm, receptor_ref),
            ]
        )
    ]
    for copy in small:
        copy.start()
    spans = [(sample, sample + 1) for sample in range(samples)]
    large = [
        pltpu.make_async_copy(x_hbm.at[pl.ds(a, b - a)], x_ref.at[pl.ds(a, b - a)], x_sem.at[i])
        for i, (a, b) in enumerate(spans)
    ]
    for spot, copy in enumerate(large):
        copy.start(priority=min(spot, 1))
    small[0].wait()
    kinds = iota((clusters, CHUNK), 0).astype(F32).astype(BF16)
    one, zero = jnp.ones((), BF16), jnp.zeros((), BF16)
    for other in small[1:]:
        other.wait()
    fill_side(weight_ref, ligand_ref, receptor_ref, side_ref)
    extras = {}
    for (first, last), copy in zip(spans, large):
        members, counts = {}, {}
        for sample in range(first, last):
            count = jnp.zeros((clusters, LANES), BF16)
            for start in range(0, cells, CHUNK):
                labels = labels_ref[sample : sample + 1, start : start + CHUNK].astype(F32)
                labels = jnp.broadcast_to(labels, (16, CHUNK)).astype(BF16)
                labels = jnp.concatenate([labels] * (clusters // 16), axis=0)
                member = jnp.where(kinds == labels, one, zero)
                for lane in range(0, CHUNK, LANES):
                    count = count + member[:, lane : lane + LANES]
                members[sample, start] = member
            row = lax.dot_general(
                jnp.ones((8, LANES), BF16), count, ROW_PAIRS, preferred_element_type=F32
            ).astype(I32)
            row = jnp.where(iota((8, LANES), 0) == 0, row - (row & 255), row & 255)
            extras[sample] = row.astype(F32)
            counts[sample] = jnp.dot(
                count, jnp.ones((LANES, genes), BF16), preferred_element_type=F32
            )
        copy.wait()
        for sample in range(first, last):
            total = jnp.zeros((clusters, genes), F32)
            for start in range(0, cells, CHUNK):
                total = total + jnp.dot(
                    members[sample, start],
                    x_ref[sample, start : start + CHUNK, :],
                    preferred_element_type=F32,
                )
            level = jnp.sum(total, axis=0, keepdims=True) * (1.0 / cells)
            level = level.astype(BF16).astype(F32)
            sums_ref[sample, :clusters, :] = (total - counts[sample] * level).astype(BF16)
            extras[sample] = jnp.where(iota((8, LANES), 0) == 2, level, extras[sample])
    turned = receiver_ref[...].astype(F32).T
    packed = jnp.concatenate([turned[start : start + 8, :] for start in range(0, rank, 8)], axis=1)
    for sample, extra in extras.items():
        sums_ref[sample, clusters:, :] = jnp.concatenate([extra, packed], axis=0).astype(BF16)


def fill_side(weight_ref, ligand_ref, receptor_ref, side_ref):
    rank = weight_ref.shape[0]
    weight = weight_ref[...]
    gram = lax.dot_general(weight, weight, ROW_PAIRS, preferred_element_type=F32)
    terms = []
    for _ in range(3):
        term = gram.astype(BF16).astype(F32)
        gram = gram - term
        terms.append(term)
    terms = jnp.concatenate(terms + [jnp.zeros((rank, LANES - 3 * rank), F32)], axis=1)
    ligand, receptor = ligand_ref[...].astype(I32), receptor_ref[...].astype(I32)
    digits = [ligand >> 7, ligand & 127, receptor >> 7, receptor & 127]
    digits = [digit.astype(F32) for digit in digits]
    weight = weight.astype(F32)
    for piece in range(rank // 2):
        low = 8 * (2 * piece // 8)
        rows = [terms[2 * piece : 2 * piece + 2, :], jnp.zeros((2, LANES), F32)]
        rows = [weight[low : low + 8, :]] + digits + rows
        side_ref[piece] = jnp.concatenate(rows, axis=0).astype(BF16)


def tables_kernel(got_ref, sender_ref, side_ref, out_ref, gram_ref):
    sources = got_ref.shape[0]
    rank, clusters = sender_ref.shape
    targets, parts = out_ref.shape[0], rank // 8
    width = clusters // sources
    extras = [got_ref[source, clusters:, :].astype(F32) for source in range(sources)]
    digits = jnp.concatenate([extra[:2, :] for extra in extras], axis=0).astype(BF16)
    levels = [jnp.broadcast_to(extra[2:3, :], (2, LANES)) for extra in extras]
    levels = jnp.concatenate(levels, axis=0).astype(BF16)
    levels = jnp.concatenate([levels, jnp.ones_like(levels)], axis=1)
    known = lax.dot_general(digits, levels, (((0,), (0,)), ((), ())), preferred_element_type=F32)
    count = jnp.maximum(known[:, LANES:], 1.0)
    total = known[:, :LANES] + jnp.sum(got_ref[:, :clusters, :].astype(F32), axis=0)
    mean = (total / count).astype(BF16)
    blocks = []
    for extra in extras:
        packed = extra[8:, :]
        pieces = [packed[:, start : start + width] for start in range(0, LANES, width)]
        blocks.append(jnp.concatenate(pieces, axis=0))
    receiver = jnp.concatenate(blocks, axis=1).astype(BF16)
    sender = sender_ref[...]
    tables = jnp.dot(jnp.concatenate([sender, receiver], axis=0), mean, preferred_element_type=F32)
    own = lax.axis_index("recv")
    lines = targets // parts
    for part in range(parts):
        low = part * 8
        both = [tables[low : low + 8, :], tables[rank + low : rank + low + 8, :]]
        both = jnp.concatenate(both, axis=0).astype(BF16)
        for line in range(lines):
            out_ref[line * parts + part, :16, :] = both
            out_ref[line * parts + part, 16:, :] = side_ref[part * 4 + (line + own) % 4]
    sender_gram = lax.dot_general(sender, sender, ROW_PAIRS, preferred_element_type=F32)
    receiver_gram = lax.dot_general(receiver, receiver, ROW_PAIRS, preferred_element_type=F32)
    gram_ref[...] = sender_gram * receiver_gram


def choose(values, which):
    bit = 1
    while len(values) > 1:
        odd = (which & bit) != 0
        values = [jnp.where(odd, b, a) for a, b in zip(values[::2], values[1::2])]
        bit *= 2
    return values[0]


def product_kernel(rank, got_ref, out_ref):
    sources = got_ref.shape[0]
    order = [line * 4 + part for part in range(4) for line in range(sources // 4)]
    tables = [got_ref[source, :16, :].astype(F32) for source in order]
    product = jnp.zeros((8, LANES), F32)
    terms = jnp.zeros((8, LANES), F32)
    for source in range(sources):
        side = got_ref[source, 16:32, :].astype(F32)
        terms = terms + side[8:, :]
        where = side[8:, :].astype(I32)
        digits = [jnp.broadcast_to(where[spot : spot + 1, :], (8, LANES)) for spot in range(4)]
        ligand = [jnp.take_along_axis(table[:8, :], digits[1], axis=1) for table in tables]
        receptor = [jnp.take_along_axis(table[8:, :], digits[3], axis=1) for table in tables]
        ligand, receptor = choose(ligand, digits[0]), choose(receptor, digits[2])
        product = product + ligand * receptor * side[:8, :]
    column = jnp.sum(product, axis=1, keepdims=True)
    line = jnp.where(iota((8, LANES), 1) == iota((8, LANES), 0) + 2 * rank, column, 0.0)
    line = jnp.sum(line, axis=0, keepdims=True)
    gram = terms[4:6, :rank] + terms[4:6, rank : 2 * rank] + terms[4:6, 2 * rank : 3 * rank]
    gram = [gram[:1, :], gram[1:, :], jnp.zeros((1, LANES - 2 * rank), F32)]
    line = line + jnp.concatenate(gram, axis=1)
    for target in range(out_ref.shape[0]):
        out_ref[target] = line


def solve_kernel(samples, got_ref, gram_ref, out_ref):
    rank = gram_ref.shape[0]
    parts = rank // 8
    scale = jnp.concatenate([gram_ref[...], jnp.ones((rank, LANES - rank), F32)], axis=1)
    rows, lanes = iota((8, LANES), 0), iota((8, LANES), 1)
    here = lax.axis_index("line")
    work = []
    for part in range(parts):
        block = jnp.zeros((8, LANES), F32)
        for sample in range(samples):
            line = got_ref[part * samples + sample]
            second = jnp.concatenate([line[:, rank:], line[:, :rank]], axis=1)
            both = jnp.where((rows & 1) == 0, line, second)
            piece = ((rows >> 1) == (here + sample) % 4) & (lanes < rank)
            block = jnp.where(piece, both, block)
            column = jnp.where(lanes == rows + 2 * rank, line, 0.0)
            column = jnp.sum(column, axis=1, keepdims=True)
            block = jnp.where(lanes == rank + sample, column, block)
        work.append(block * scale[8 * part : 8 * part + 8, :])
    for part in range(parts):
        columns = [
            [jnp.broadcast_to(block[:, lane : lane + 1], (8, LANES)) for block in work]
            for lane in range(8 * part, 8 * part + 8)
        ]
        lead, inner = work[part], [column[part] for column in columns]
        for row in range(8):
            pivot = inner[row][row : row + 1, :]
            pivot = jnp.where(pivot > 0.0, 1.0 / pivot, jnp.nan)
            here, times = rows == row, inner[row]
            line = lead[row : row + 1, :] * pivot
            lead = jnp.where(here, line, lead - times * line)
            for later in range(row + 1, 8):
                line = inner[later][row : row + 1, :] * pivot
                inner[later] = jnp.where(here, line, inner[later] - times * line)
        for other in range(parts):
            if other == part:
                work[other] = lead
            else:
                for row in range(8):
                    work[other] = work[other] - columns[row][other] * lead[row : row + 1, :]
    answer = jnp.concatenate(work, axis=0)[:, rank : rank + 8].T
    out_ref[...] = answer[:samples, :]


def on_chip(array):
    return pltpu.with_memory_space_constraint(array, pltpu.VMEM)


def body(
    cell_expression,
    cell_labels,
    ligand_gene,
    receptor_gene,
    pair_factor,
    sender_factor,
    receiver_factor,
):
    samples, cells, genes = cell_expression.shape
    clusters, rank = sender_factor.shape
    parts = lax.axis_size("part")
    targets = parts * lax.axis_size("line")
    anywhere = pl.BlockSpec(memory_space=pl.ANY)
    vmem = pl.BlockSpec(memory_space=pltpu.VMEM)
    sums, side, sender = pl.pallas_call(
        totals_kernel,
        in_specs=[anywhere] * 7,
        out_specs=(vmem, vmem, vmem),
        out_shape=(
            pltpu.VMEM((samples, clusters + 16, genes), BF16),
            pltpu.VMEM((rank // 2, 16, LANES), BF16),
            pltpu.VMEM((rank, clusters), BF16),
        ),
        scratch_shapes=[
            pltpu.VMEM((samples, cells, genes), BF16),
            pltpu.VMEM((samples, cells), I32),
            pltpu.VMEM(receiver_factor.shape, BF16),
            pltpu.VMEM((rank, LANES), BF16),
            pltpu.VMEM((1, LANES), I32),
            pltpu.VMEM((1, LANES), I32),
            pltpu.SemaphoreType.DMA((samples,)),
            pltpu.SemaphoreType.DMA((6,)),
        ],
        name="totals",
    )(
        cell_expression,
        cell_labels,
        receiver_factor,
        sender_factor.T,
        pair_factor.T,
        ligand_gene[None, :],
        receptor_gene[None, :],
    )
    side, sender = on_chip(side), on_chip(sender)
    got = on_chip(lax.all_to_all(sums, "recv", 0, 0, tiled=True))
    sent, gram = pl.pallas_call(
        tables_kernel,
        in_specs=[vmem] * 3,
        out_specs=(vmem, vmem),
        out_shape=(
            pltpu.VMEM((targets, 32, genes), BF16),
            pltpu.VMEM((rank, rank), F32),
        ),
        name="tables",
    )(got, sender, side)
    got = on_chip(lax.all_to_all(sent, ("line", "part"), 0, 0, tiled=True))
    sent = pl.pallas_call(
        lambda *refs: product_kernel(rank, *refs),
        in_specs=[vmem],
        out_specs=vmem,
        out_shape=pltpu.VMEM((parts * samples, 1, LANES), F32),
        name="product",
    )(got)
    got = on_chip(lax.all_to_all(sent, ("part", "recv"), 0, 0, tiled=True))
    return pl.pallas_call(
        lambda *refs: solve_kernel(samples, *refs),
        in_specs=[vmem] * 2,
        out_specs=vmem,
        out_shape=jax.ShapeDtypeStruct((samples, rank), F32),
        name="solve",
    )(got, on_chip(gram))


def solution(mesh):
    samp, pair, recv = mesh.devices.shape
    split = Mesh(mesh.devices.reshape(samp, 4, pair // 4, recv), ("samp", "part", "line", "recv"))
    pairs = ("part", "line")
    placed = (
        P("samp", "recv", pairs),
        P("samp", "recv"),
        P(pairs),
        P(pairs),
        P(pairs, None),
        P(),
        P("recv", None),
    )
    return jax.shard_map(
        body, mesh=split, in_specs=placed, out_specs=P("samp", None), check_vma=False
    )
```

```python
import jax
import jax.numpy as jnp
from jax import lax
from jax.experimental import pallas as pl
from jax.experimental.pallas import tpu as pltpu
from jax.sharding import Mesh
from jax.sharding import PartitionSpec as P

F32 = jnp.float32
BF16 = jnp.bfloat16
I32 = jnp.int32
LANES = 128
CHUNK = 512
ROW_PAIRS = (((1,), (1,)), ((), ()))


def iota(shape, dim):
    return lax.broadcasted_iota(I32, shape, dim)


def totals_kernel(
    x_hbm, labels_hbm, receiver_hbm, sender_hbm, weight_hbm, ligand_hbm, receptor_hbm,
    sums_ref, side_ref, sender_ref,
    x_ref, labels_ref, receiver_ref, weight_ref, ligand_ref, receptor_ref, x_sem, sems,
):
    samples, cells, genes = x_ref.shape
    rank, clusters = sender_ref.shape
    small = [
        pltpu.make_async_copy(source, target, sems.at[spot])
        for spot, (source, target) in enumerate(
            [
                (labels_hbm, labels_ref),
                (receiver_hbm, receiver_ref),
                (sender_hbm, sender_ref),
                (weight_hbm, weight_ref),
                (ligand_hbm, ligand_ref),
                (receptor_hbm, receptor_ref),
            ]
        )
    ]
    for copy in small:
        copy.start()
    spans = [(sample, sample + 1) for sample in range(samples)]
    large = [
        pltpu.make_async_copy(x_hbm.at[pl.ds(a, b - a)], x_ref.at[pl.ds(a, b - a)], x_sem.at[i])
        for i, (a, b) in enumerate(spans)
    ]
    for spot, copy in enumerate(large):
        copy.start(priority=min(spot, 1))
    small[0].wait()
    kinds = iota((clusters, CHUNK), 0).astype(F32).astype(BF16)
    one, zero = jnp.ones((), BF16), jnp.zeros((), BF16)
    for other in small[1:]:
        other.wait()
    fill_side(weight_ref, ligand_ref, receptor_ref, side_ref)
    extras = {}
    for (first, last), copy in zip(spans, large):
        members, counts = {}, {}
        for sample in range(first, last):
            count = jnp.zeros((clusters, LANES), BF16)
            for start in range(0, cells, CHUNK):
                labels = labels_ref[sample : sample + 1, start : start + CHUNK].astype(F32)
                labels = jnp.broadcast_to(labels, (16, CHUNK)).astype(BF16)
                labels = jnp.concatenate([labels] * (clusters // 16), axis=0)
                member = jnp.where(kinds == labels, one, zero)
                for lane in range(0, CHUNK, LANES):
                    count = count + member[:, lane : lane + LANES]
                members[sample, start] = member
            row = lax.dot_general(
                jnp.ones((8, LANES), BF16), count, ROW_PAIRS, preferred_element_type=F32
            ).astype(I32)
            row = jnp.where(iota((8, LANES), 0) == 0, row - (row & 255), row & 255)
            extras[sample] = row.astype(F32)
            counts[sample] = jnp.dot(
                count, jnp.ones((LANES, genes), BF16), preferred_element_type=F32
            )
        copy.wait()
        for sample in range(first, last):
            total = jnp.zeros((clusters, genes), F32)
            for start in range(0, cells, CHUNK):
                total = total + jnp.dot(
                    members[sample, start],
                    x_ref[sample, start : start + CHUNK, :],
                    preferred_element_type=F32,
                )
            level = jnp.sum(total, axis=0, keepdims=True) * (1.0 / cells)
            level = level.astype(BF16).astype(F32)
            sums_ref[sample, :clusters, :] = (total - counts[sample] * level).astype(BF16)
            extras[sample] = jnp.where(iota((8, LANES), 0) == 2, level, extras[sample])
    turned = receiver_ref[...].astype(F32).T
    packed = jnp.concatenate([turned[start : start + 8, :] for start in range(0, rank, 8)], axis=1)
    for sample, extra in extras.items():
        sums_ref[sample, clusters:, :] = jnp.concatenate([extra, packed], axis=0).astype(BF16)


def fill_side(weight_ref, ligand_ref, receptor_ref, side_ref):
    rank = weight_ref.shape[0]
    weight = weight_ref[...]
    gram = lax.dot_general(weight, weight, ROW_PAIRS, preferred_element_type=F32)
    terms = []
    for _ in range(3):
        term = gram.astype(BF16).astype(F32)
        gram = gram - term
        terms.append(term)
    terms = jnp.concatenate(terms + [jnp.zeros((rank, LANES - 3 * rank), F32)], axis=1)
    ligand, receptor = ligand_ref[...].astype(I32), receptor_ref[...].astype(I32)
    digits = [ligand >> 7, ligand & 127, receptor >> 7, receptor & 127]
    digits = [digit.astype(F32) for digit in digits]
    weight = weight.astype(F32)
    for piece in range(rank // 2):
        low = 8 * (2 * piece // 8)
        rows = [terms[2 * piece : 2 * piece + 2, :], jnp.zeros((2, LANES), F32)]
        rows = [weight[low : low + 8, :]] + digits + rows
        side_ref[piece] = jnp.concatenate(rows, axis=0).astype(BF16)


def tables_kernel(got_ref, sender_ref, side_ref, out_ref, gram_ref):
    sources = got_ref.shape[0]
    rank, clusters = sender_ref.shape
    targets, parts = out_ref.shape[0], rank // 8
    width = clusters // sources
    extras = [got_ref[source, clusters:, :].astype(F32) for source in range(sources)]
    digits = jnp.concatenate([extra[:2, :] for extra in extras], axis=0).astype(BF16)
    levels = [jnp.broadcast_to(extra[2:3, :], (2, LANES)) for extra in extras]
    levels = jnp.concatenate(levels, axis=0).astype(BF16)
    levels = jnp.concatenate([levels, jnp.ones_like(levels)], axis=1)
    known = lax.dot_general(digits, levels, (((0,), (0,)), ((), ())), preferred_element_type=F32)
    count = jnp.maximum(known[:, LANES:], 1.0)
    total = known[:, :LANES] + jnp.sum(got_ref[:, :clusters, :].astype(F32), axis=0)
    mean = (total / count).astype(BF16)
    blocks = []
    for extra in extras:
        packed = extra[8:, :]
        pieces = [packed[:, start : start + width] for start in range(0, LANES, width)]
        blocks.append(jnp.concatenate(pieces, axis=0))
    receiver = jnp.concatenate(blocks, axis=1).astype(BF16)
    sender = sender_ref[...]
    tables = jnp.dot(jnp.concatenate([sender, receiver], axis=0), mean, preferred_element_type=F32)
    own = lax.axis_index("recv")
    lines = targets // parts
    for part in range(parts):
        low = part * 8
        both = [tables[low : low + 8, :], tables[rank + low : rank + low + 8, :]]
        both = jnp.concatenate(both, axis=0).astype(BF16)
        for line in range(lines):
            out_ref[line * parts + part, :16, :] = both
            out_ref[line * parts + part, 16:, :] = side_ref[part * 4 + (line + own) % 4]
    sender_gram = lax.dot_general(sender, sender, ROW_PAIRS, preferred_element_type=F32)
    receiver_gram = lax.dot_general(receiver, receiver, ROW_PAIRS, preferred_element_type=F32)
    gram_ref[...] = sender_gram * receiver_gram


def choose(values, which):
    bit = 1
    while len(values) > 1:
        odd = (which & bit) != 0
        values = [jnp.where(odd, b, a) for a, b in zip(values[::2], values[1::2])]
        bit *= 2
    return values[0]


def product_kernel(rank, got_ref, out_ref):
    sources = got_ref.shape[0]
    order = [line * 4 + part for part in range(4) for line in range(sources // 4)]
    tables = [got_ref[source, :16, :].astype(F32) for source in order]
    product = jnp.zeros((8, LANES), F32)
    terms = jnp.zeros((8, LANES), F32)
    for source in range(sources):
        side = got_ref[source, 16:32, :].astype(F32)
        terms = terms + side[8:, :]
        where = side[8:, :].astype(I32)
        digits = [jnp.broadcast_to(where[spot : spot + 1, :], (8, LANES)) for spot in range(4)]
        ligand = [jnp.take_along_axis(table[:8, :], digits[1], axis=1) for table in tables]
        receptor = [jnp.take_along_axis(table[8:, :], digits[3], axis=1) for table in tables]
        ligand, receptor = choose(ligand, digits[0]), choose(receptor, digits[2])
        product = product + ligand * receptor * side[:8, :]
    column = jnp.sum(product, axis=1, keepdims=True)
    line = jnp.where(iota((8, LANES), 1) == iota((8, LANES), 0) + 2 * rank, column, 0.0)
    line = jnp.sum(line, axis=0, keepdims=True)
    gram = terms[4:6, :rank] + terms[4:6, rank : 2 * rank] + terms[4:6, 2 * rank : 3 * rank]
    gram = [gram[:1, :], gram[1:, :], jnp.zeros((1, LANES - 2 * rank), F32)]
    line = line + jnp.concatenate(gram, axis=1)
    for target in range(out_ref.shape[0]):
        out_ref[target] = line


def total_of(terms):
    while len(terms) > 1:
        rest = terms[len(terms) // 2 * 2 :]
        terms = [a + b for a, b in zip(terms[::2], terms[1::2])] + rest
    return terms[0]


def solve_kernel(samples, got_ref, gram_ref, out_ref):
    rank = gram_ref.shape[0]
    parts = rank // 8
    scale = jnp.concatenate([gram_ref[...], jnp.ones((rank, LANES - rank), F32)], axis=1)
    rows = iota((8, LANES), 0)
    line = lax.axis_index("line")
    first = jnp.concatenate([got_ref[source] for source in range(parts * samples)], axis=0)
    second = jnp.concatenate([first[:, rank:], first[:, :rank]], axis=1)
    right = first.T[2 * rank : 2 * rank + 8, :]
    work = []
    for part in range(parts):
        low = part * samples
        block = jnp.zeros((8, rank), F32)
        for sample in range(samples):
            at = low + sample
            both = jnp.where((rows & 1) == 0, first[at : at + 1, :], second[at : at + 1, :])
            piece = (rows >> 1)[:, :rank] == (line + sample) % 4
            block = jnp.where(piece, both[:, :rank], block)
        rest = jnp.zeros((8, LANES - rank - samples), F32)
        block = jnp.concatenate([block, right[:, low : low + samples], rest], axis=1)
        work.append(block * scale[8 * part : 8 * part + 8, :])
    for part in range(parts):
        spread = [
            [jnp.broadcast_to(block[:, lane : lane + 1], (8, LANES)) for block in work[part:]]
            for lane in range(8 * part, 8 * part + 8)
        ]
        lead, inner = work[part], [column[0] for column in spread]
        for row in range(8):
            pivot = inner[row][row : row + 1, :]
            pivot = jnp.where(pivot > 0.0, 1.0 / pivot, jnp.nan)
            here, times = rows == row, inner[row]
            line = lead[row : row + 1, :] * pivot
            lead = jnp.where(here, line, lead - times * line)
            for later in range(row + 1, 8):
                line = inner[later][row : row + 1, :] * pivot
                inner[later] = jnp.where(here, line, inner[later] - times * line)
        work[part] = lead
        for other in range(part + 1, parts):
            terms = [spread[row][other - part] * lead[row : row + 1, :] for row in range(8)]
            work[other] = work[other] - total_of(terms)
    for part in range(parts - 2, -1, -1):
        terms = [
            jnp.broadcast_to(work[part][:, lane : lane + 1], (8, LANES))
            * work[lane // 8][lane % 8 : lane % 8 + 1, :]
            for lane in range(8 * part + 8, rank)
        ]
        work[part] = work[part] - total_of(terms)
    answer = jnp.concatenate(work, axis=0)[:, rank : rank + 8].T
    out_ref[...] = answer[:samples, :]


def on_chip(array):
    return pltpu.with_memory_space_constraint(array, pltpu.VMEM)


def body(
    cell_expression,
    cell_labels,
    ligand_gene,
    receptor_gene,
    pair_factor,
    sender_factor,
    receiver_factor,
):
    samples, cells, genes = cell_expression.shape
    clusters, rank = sender_factor.shape
    parts = lax.axis_size("part")
    targets = parts * lax.axis_size("line")
    anywhere = pl.BlockSpec(memory_space=pl.ANY)
    vmem = pl.BlockSpec(memory_space=pltpu.VMEM)
    sums, side, sender = pl.pallas_call(
        totals_kernel,
        in_specs=[anywhere] * 7,
        out_specs=(vmem, vmem, vmem),
        out_shape=(
            pltpu.VMEM((samples, clusters + 16, genes), BF16),
            pltpu.VMEM((rank // 2, 16, LANES), BF16),
            pltpu.VMEM((rank, clusters), BF16),
        ),
        scratch_shapes=[
            pltpu.VMEM((samples, cells, genes), BF16),
            pltpu.VMEM((samples, cells), I32),
            pltpu.VMEM(receiver_factor.shape, BF16),
            pltpu.VMEM((rank, LANES), BF16),
            pltpu.VMEM((1, LANES), I32),
            pltpu.VMEM((1, LANES), I32),
            pltpu.SemaphoreType.DMA((samples,)),
            pltpu.SemaphoreType.DMA((6,)),
        ],
        name="totals",
    )(
        cell_expression,
        cell_labels,
        receiver_factor,
        sender_factor.T,
        pair_factor.T,
        ligand_gene[None, :],
        receptor_gene[None, :],
    )
    side, sender = on_chip(side), on_chip(sender)
    got = on_chip(lax.all_to_all(sums, "recv", 0, 0, tiled=True))
    sent, gram = pl.pallas_call(
        tables_kernel,
        in_specs=[vmem] * 3,
        out_specs=(vmem, vmem),
        out_shape=(
            pltpu.VMEM((targets, 32, genes), BF16),
            pltpu.VMEM((rank, rank), F32),
        ),
        name="tables",
    )(got, sender, side)
    got = on_chip(lax.all_to_all(sent, ("line", "part"), 0, 0, tiled=True))
    sent = pl.pallas_call(
        lambda *refs: product_kernel(rank, *refs),
        in_specs=[vmem],
        out_specs=vmem,
        out_shape=pltpu.VMEM((parts * samples, 1, LANES), F32),
        name="product",
    )(got)
    got = on_chip(lax.all_to_all(sent, ("part", "recv"), 0, 0, tiled=True))
    return pl.pallas_call(
        lambda *refs: solve_kernel(samples, *refs),
        in_specs=[vmem] * 2,
        out_specs=vmem,
        out_shape=jax.ShapeDtypeStruct((samples, rank), F32),
        name="solve",
    )(got, on_chip(gram))


def solution(mesh):
    samp, pair, recv = mesh.devices.shape
    split = Mesh(mesh.devices.reshape(samp, 4, pair // 4, recv), ("samp", "part", "line", "recv"))
    pairs = ("part", "line")
    placed = (
        P("samp", "recv", pairs),
        P("samp", "recv"),
        P(pairs),
        P(pairs),
        P(pairs, None),
        P(),
        P("recv", None),
    )
    return jax.shard_map(
        body, mesh=split, in_specs=placed, out_specs=P("samp", None), check_vma=False
    )
```

```python
import jax
import jax.numpy as jnp
from jax import lax
from jax.experimental import pallas as pl
from jax.experimental.pallas import tpu as pltpu
from jax.sharding import Mesh
from jax.sharding import PartitionSpec as P

F32 = jnp.float32
BF16 = jnp.bfloat16
I32 = jnp.int32
LANES = 128
CHUNK = 512
ROW_PAIRS = (((1,), (1,)), ((), ()))


def iota(shape, dim):
    return lax.broadcasted_iota(I32, shape, dim)


def totals_kernel(
    x_hbm, labels_hbm, receiver_hbm, sender_hbm, weight_hbm, ligand_hbm, receptor_hbm,
    sums_ref, side_ref, sender_ref,
    x_ref, labels_ref, receiver_ref, weight_ref, ligand_ref, receptor_ref, x_sem, sems,
):
    samples, cells, genes = x_ref.shape
    rank, clusters = sender_ref.shape
    small = [
        pltpu.make_async_copy(source, target, sems.at[spot])
        for spot, (source, target) in enumerate(
            [
                (labels_hbm, labels_ref),
                (receiver_hbm, receiver_ref),
                (sender_hbm, sender_ref),
                (weight_hbm, weight_ref),
                (ligand_hbm, ligand_ref),
                (receptor_hbm, receptor_ref),
            ]
        )
    ]
    for copy in small:
        copy.start()
    spans = [(sample, sample + 1) for sample in range(samples)]
    large = [
        pltpu.make_async_copy(x_hbm.at[pl.ds(a, b - a)], x_ref.at[pl.ds(a, b - a)], x_sem.at[i])
        for i, (a, b) in enumerate(spans)
    ]
    for spot, copy in enumerate(large):
        copy.start(priority=min(spot // 2, 1))
    small[0].wait()
    kinds = iota((clusters, CHUNK), 0).astype(F32).astype(BF16)
    one, zero = jnp.ones((), BF16), jnp.zeros((), BF16)
    for other in small[1:]:
        other.wait()
    fill_side(weight_ref, ligand_ref, receptor_ref, side_ref)
    extras = {}
    for (first, last), copy in zip(spans, large):
        members, counts = {}, {}
        for sample in range(first, last):
            count = jnp.zeros((clusters, LANES), BF16)
            for start in range(0, cells, CHUNK):
                labels = labels_ref[sample : sample + 1, start : start + CHUNK].astype(F32)
                labels = jnp.broadcast_to(labels, (16, CHUNK)).astype(BF16)
                labels = jnp.concatenate([labels] * (clusters // 16), axis=0)
                member = jnp.where(kinds == labels, one, zero)
                for lane in range(0, CHUNK, LANES):
                    count = count + member[:, lane : lane + LANES]
                members[sample, start] = member
            row = lax.dot_general(
                jnp.ones((8, LANES), BF16), count, ROW_PAIRS, preferred_element_type=F32
            ).astype(I32)
            row = jnp.where(iota((8, LANES), 0) == 0, row - (row & 255), row & 255)
            extras[sample] = row.astype(F32)
            counts[sample] = jnp.dot(
                count, jnp.ones((LANES, genes), BF16), preferred_element_type=F32
            )
        copy.wait()
        for sample in range(first, last):
            total = jnp.zeros((clusters, genes), F32)
            for start in range(0, cells, CHUNK):
                total = total + jnp.dot(
                    members[sample, start],
                    x_ref[sample, start : start + CHUNK, :],
                    preferred_element_type=F32,
                )
            level = jnp.sum(total, axis=0, keepdims=True) * (1.0 / cells)
            level = level.astype(BF16).astype(F32)
            sums_ref[sample, :clusters, :] = (total - counts[sample] * level).astype(BF16)
            extras[sample] = jnp.where(iota((8, LANES), 0) == 2, level, extras[sample])
    turned = receiver_ref[...].astype(F32).T
    packed = jnp.concatenate([turned[start : start + 8, :] for start in range(0, rank, 8)], axis=1)
    for sample, extra in extras.items():
        sums_ref[sample, clusters:, :] = jnp.concatenate([extra, packed], axis=0).astype(BF16)


def fill_side(weight_ref, ligand_ref, receptor_ref, side_ref):
    rank = weight_ref.shape[0]
    weight = weight_ref[...]
    gram = lax.dot_general(weight, weight, ROW_PAIRS, preferred_element_type=F32)
    terms = []
    for _ in range(3):
        term = gram.astype(BF16).astype(F32)
        gram = gram - term
        terms.append(term)
    terms = jnp.concatenate(terms + [jnp.zeros((rank, LANES - 3 * rank), F32)], axis=1)
    ligand, receptor = ligand_ref[...].astype(I32), receptor_ref[...].astype(I32)
    digits = [ligand >> 7, ligand & 127, receptor >> 7, receptor & 127]
    digits = [digit.astype(F32) for digit in digits]
    weight = weight.astype(F32)
    for piece in range(rank // 2):
        low = 8 * (2 * piece // 8)
        rows = [terms[2 * piece : 2 * piece + 2, :], jnp.zeros((2, LANES), F32)]
        rows = [weight[low : low + 8, :]] + digits + rows
        side_ref[piece] = jnp.concatenate(rows, axis=0).astype(BF16)


def tables_kernel(got_ref, sender_ref, side_ref, out_ref, gram_ref):
    sources = got_ref.shape[0]
    rank, clusters = sender_ref.shape
    targets, parts = out_ref.shape[0], rank // 8
    width = clusters // sources
    extras = [got_ref[source, clusters:, :].astype(F32) for source in range(sources)]
    digits = jnp.concatenate([extra[:2, :] for extra in extras], axis=0).astype(BF16)
    levels = [jnp.broadcast_to(extra[2:3, :], (2, LANES)) for extra in extras]
    levels = jnp.concatenate(levels, axis=0).astype(BF16)
    levels = jnp.concatenate([levels, jnp.ones_like(levels)], axis=1)
    known = lax.dot_general(digits, levels, (((0,), (0,)), ((), ())), preferred_element_type=F32)
    count = jnp.maximum(known[:, LANES:], 1.0)
    total = known[:, :LANES] + jnp.sum(got_ref[:, :clusters, :].astype(F32), axis=0)
    mean = (total / count).astype(BF16)
    blocks = []
    for extra in extras:
        packed = extra[8:, :]
        pieces = [packed[:, start : start + width] for start in range(0, LANES, width)]
        blocks.append(jnp.concatenate(pieces, axis=0))
    receiver = jnp.concatenate(blocks, axis=1).astype(BF16)
    sender = sender_ref[...]
    tables = jnp.dot(jnp.concatenate([sender, receiver], axis=0), mean, preferred_element_type=F32)
    own = lax.axis_index("recv")
    lines = targets // parts
    for part in range(parts):
        low = part * 8
        both = [tables[low : low + 8, :], tables[rank + low : rank + low + 8, :]]
        both = jnp.concatenate(both, axis=0).astype(BF16)
        for line in range(lines):
            out_ref[line * parts + part, :16, :] = both
            out_ref[line * parts + part, 16:, :] = side_ref[part * 4 + (line + own) % 4]
    sender_gram = lax.dot_general(sender, sender, ROW_PAIRS, preferred_element_type=F32)
    receiver_gram = lax.dot_general(receiver, receiver, ROW_PAIRS, preferred_element_type=F32)
    gram_ref[...] = sender_gram * receiver_gram


def choose(values, which):
    bit = 1
    while len(values) > 1:
        odd = (which & bit) != 0
        values = [jnp.where(odd, b, a) for a, b in zip(values[::2], values[1::2])]
        bit *= 2
    return values[0]


def product_kernel(rank, got_ref, out_ref):
    sources = got_ref.shape[0]
    order = [line * 4 + part for part in range(4) for line in range(sources // 4)]
    tables = [got_ref[source, :16, :].astype(F32) for source in order]
    product = jnp.zeros((8, LANES), F32)
    terms = jnp.zeros((8, LANES), F32)
    for source in range(sources):
        side = got_ref[source, 16:32, :].astype(F32)
        terms = terms + side[8:, :]
        where = side[8:, :].astype(I32)
        digits = [jnp.broadcast_to(where[spot : spot + 1, :], (8, LANES)) for spot in range(4)]
        ligand = [jnp.take_along_axis(table[:8, :], digits[1], axis=1) for table in tables]
        receptor = [jnp.take_along_axis(table[8:, :], digits[3], axis=1) for table in tables]
        ligand, receptor = choose(ligand, digits[0]), choose(receptor, digits[2])
        product = product + ligand * receptor * side[:8, :]
    column = jnp.sum(product, axis=1, keepdims=True)
    line = jnp.where(iota((8, LANES), 1) == iota((8, LANES), 0) + 2 * rank, column, 0.0)
    line = jnp.sum(line, axis=0, keepdims=True)
    gram = terms[4:6, :rank] + terms[4:6, rank : 2 * rank] + terms[4:6, 2 * rank : 3 * rank]
    gram = [gram[:1, :], gram[1:, :], jnp.zeros((1, LANES - 2 * rank), F32)]
    line = line + jnp.concatenate(gram, axis=1)
    for target in range(out_ref.shape[0]):
        out_ref[target] = line


def total_of(terms):
    while len(terms) > 1:
        rest = terms[len(terms) // 2 * 2 :]
        terms = [a + b for a, b in zip(terms[::2], terms[1::2])] + rest
    return terms[0]


def solve_kernel(samples, got_ref, gram_ref, out_ref):
    rank = gram_ref.shape[0]
    parts = rank // 8
    scale = jnp.concatenate([gram_ref[...], jnp.ones((rank, LANES - rank), F32)], axis=1)
    rows = iota((8, LANES), 0)
    line = lax.axis_index("line")
    first = jnp.concatenate([got_ref[source] for source in range(parts * samples)], axis=0)
    second = jnp.concatenate([first[:, rank:], first[:, :rank]], axis=1)
    right = first.T[2 * rank : 2 * rank + 8, :]
    work = []
    for part in range(parts):
        low = part * samples
        block = jnp.zeros((8, rank), F32)
        for sample in range(samples):
            at = low + sample
            both = jnp.where((rows & 1) == 0, first[at : at + 1, :], second[at : at + 1, :])
            piece = (rows >> 1)[:, :rank] == (line + sample) % 4
            block = jnp.where(piece, both[:, :rank], block)
        rest = jnp.zeros((8, LANES - rank - samples), F32)
        block = jnp.concatenate([block, right[:, low : low + samples], rest], axis=1)
        work.append(block * scale[8 * part : 8 * part + 8, :])
    for part in range(parts):
        spread = [
            [jnp.broadcast_to(block[:, lane : lane + 1], (8, LANES)) for block in work[part:]]
            for lane in range(8 * part, 8 * part + 8)
        ]
        lead, inner = work[part], [column[0] for column in spread]
        for row in range(8):
            pivot = inner[row][row : row + 1, :]
            pivot = jnp.where(pivot > 0.0, 1.0 / pivot, jnp.nan)
            here, times = rows == row, inner[row]
            line = lead[row : row + 1, :] * pivot
            lead = jnp.where(here, line, lead - times * line)
            for later in range(row + 1, 8):
                line = inner[later][row : row + 1, :] * pivot
                inner[later] = jnp.where(here, line, inner[later] - times * line)
        work[part] = lead
        for other in range(part + 1, parts):
            terms = [spread[row][other - part] * lead[row : row + 1, :] for row in range(8)]
            work[other] = work[other] - total_of(terms)
    for part in range(parts - 2, -1, -1):
        terms = [
            jnp.broadcast_to(work[part][:, lane : lane + 1], (8, LANES))
            * work[lane // 8][lane % 8 : lane % 8 + 1, :]
            for lane in range(8 * part + 8, rank)
        ]
        work[part] = work[part] - total_of(terms)
    answer = jnp.concatenate(work, axis=0)[:, rank : rank + 8].T
    out_ref[...] = answer[:samples, :]


def on_chip(array):
    return pltpu.with_memory_space_constraint(array, pltpu.VMEM)


def body(
    cell_expression,
    cell_labels,
    ligand_gene,
    receptor_gene,
    pair_factor,
    sender_factor,
    receiver_factor,
):
    samples, cells, genes = cell_expression.shape
    clusters, rank = sender_factor.shape
    parts = lax.axis_size("part")
    targets = parts * lax.axis_size("line")
    anywhere = pl.BlockSpec(memory_space=pl.ANY)
    vmem = pl.BlockSpec(memory_space=pltpu.VMEM)
    sums, side, sender = pl.pallas_call(
        totals_kernel,
        in_specs=[anywhere] * 7,
        out_specs=(vmem, vmem, vmem),
        out_shape=(
            pltpu.VMEM((samples, clusters + 16, genes), BF16),
            pltpu.VMEM((rank // 2, 16, LANES), BF16),
            pltpu.VMEM((rank, clusters), BF16),
        ),
        scratch_shapes=[
            pltpu.VMEM((samples, cells, genes), BF16),
            pltpu.VMEM((samples, cells), I32),
            pltpu.VMEM(receiver_factor.shape, BF16),
            pltpu.VMEM((rank, LANES), BF16),
            pltpu.VMEM((1, LANES), I32),
            pltpu.VMEM((1, LANES), I32),
            pltpu.SemaphoreType.DMA((samples,)),
            pltpu.SemaphoreType.DMA((6,)),
        ],
        name="totals",
    )(
        cell_expression,
        cell_labels,
        receiver_factor,
        sender_factor.T,
        pair_factor.T,
        ligand_gene[None, :],
        receptor_gene[None, :],
    )
    side, sender = on_chip(side), on_chip(sender)
    got = on_chip(lax.all_to_all(sums, "recv", 0, 0, tiled=True))
    sent, gram = pl.pallas_call(
        tables_kernel,
        in_specs=[vmem] * 3,
        out_specs=(vmem, vmem),
        out_shape=(
            pltpu.VMEM((targets, 32, genes), BF16),
            pltpu.VMEM((rank, rank), F32),
        ),
        name="tables",
    )(got, sender, side)
    got = on_chip(lax.all_to_all(sent, ("line", "part"), 0, 0, tiled=True))
    sent = pl.pallas_call(
        lambda *refs: product_kernel(rank, *refs),
        in_specs=[vmem],
        out_specs=vmem,
        out_shape=pltpu.VMEM((parts * samples, 1, LANES), F32),
        name="product",
    )(got)
    got = on_chip(lax.all_to_all(sent, ("part", "recv"), 0, 0, tiled=True))
    return pl.pallas_call(
        lambda *refs: solve_kernel(samples, *refs),
        in_specs=[vmem] * 2,
        out_specs=vmem,
        out_shape=jax.ShapeDtypeStruct((samples, rank), F32),
        name="solve",
    )(got, on_chip(gram))


def solution(mesh):
    samp, pair, recv = mesh.devices.shape
    split = Mesh(mesh.devices.reshape(samp, 4, pair // 4, recv), ("samp", "part", "line", "recv"))
    pairs = ("part", "line")
    placed = (
        P("samp", "recv", pairs),
        P("samp", "recv"),
        P(pairs),
        P(pairs),
        P(pairs, None),
        P(),
        P("recv", None),
    )
    return jax.shard_map(
        body, mesh=split, in_specs=placed, out_specs=P("samp", None), check_vma=False
    )
```
